32 devices in a mesh: grp: 2 (over y), row: 4 (over z), col: 4 (over x, core).
Axes of the slice: x: 2, y: 2, z: 4, core: 2. Of those that a mesh axis runs over, the one named last changes fastest.
Arguments:
- inputs: bfloat16 [256, 16384], P(('grp', 'row'), 'col'), parts along dimension 0, may hold values from -6 to 6
- output_gradient: bfloat16 [256, 16384], P(('grp', 'row'), 'col'), parts along dimension 0, may hold values from -6 to 6
- gate_preactivation: bfloat16 [256, 8192], P('grp', 'row'), parts along dimension 0, may hold values from -6 to 6
- up_preactivation: bfloat16 [256, 8192], P('grp', 'row'), parts along dimension 0, may hold values from -6 to 6
- gate_weight: bfloat16 [16384, 8192], P('col', 'row'), may hold values from -0.046875 to 0.046875
- up_weight: bfloat16 [16384, 8192], P('col', 'row'), may hold values from -0.046875 to 0.046875
- down_weight: bfloat16 [8192, 16384], P('row', 'col'), may hold values from -0.0625 to 0.0625
- up_adapter_entry: bfloat16 [16, 16384], P(None, 'col'), may hold values from -6 to 6
- up_adapter_exit: bfloat16 [16, 8192], P(None, 'row'), may hold values from -0.0032958984 to 0.0032958984
- down_adapter_entry: bfloat16 [16, 8192], P(None, 'row'), may hold values from -6 to 6
- down_adapter_exit: bfloat16 [16, 16384], P(None, 'col'), may hold values from -0.0023956299 to 0.0023956299
- up_adapter_activations: bfloat16 [16, 256], P(None, 'grp'), parts along dimension 1, may hold values from -0.29882812 to 0.29882812
- down_adapter_activations: bfloat16 [16, 256], P(None, 'grp'), parts along dimension 1, may hold values from -0.29882812 to 0.29882812
Outputs:
- grad_inputs: bfloat16 [256, 16384], P(('grp', 'row'), 'col'), parts along dimension 0
- up_entry_gradient: float32 [32, 16384], P('grp', 'col'), parts along dimension 0
- up_exit_gradient: float32 [32, 8192], P('grp', 'row'), parts along dimension 0
- down_entry_gradient: float32 [32, 8192], P('grp', 'row'), parts along dimension 0
- down_exit_gradient: float32 [32, 16384], P('grp', 'col'), parts along dimension 0
The draws below stay inside these ranges and needn't reach their ends.
There are 2 independent parts, one for each index of `grp`. The reference program is written for one: setup_inputs(seed, part) draws one part's arguments, and reference() takes and returns one part's arrays. A program takes and returns all parts, laid end to end along the dimension named above; an argument that names none is the same for every part. Nothing has to cross between parts.
All inputs are finite; a program needn't handle non-finite values.
Results may differ from the reference program's by a relative error of at most 0.005.
Values may be sent and summed in bfloat16 or wider, within the bound.
No kernel may reach another device: no remote copies, remote signals or barrier semaphores. Data moves between devices by JAX's collectives and lax.ppermute only.
A program may use at most 128 MiB of HBM per device.

```python
import jax
import jax.numpy as jnp
from jax import lax

MODEL_WIDTH = 16384
HIDDEN_COUNT = 8192
ADAPTER_RANK = 16
TOKENS = 128


def spiked(entries, stream_key, source, target, shards_of, factor):
    def block_of(position):
        return (jnp.arange(entries.shape[position]) // (entries.shape[position] // shards_of)).reshape((-1,) + (1,) * (entries.ndim - 1 - position))

    one_side = jax.random.permutation(stream_key, shards_of)[block_of(target)]
    other_side = (block_of(target) + shards_of // 2) % shards_of
    return jnp.where((block_of(source) == one_side) | (block_of(source) == other_side), factor * entries, entries)


def levels(rng, shape, split, low, top_value):
    factor_of, own = 1.0, jax.random.fold_in(rng, 6)
    for position, blocks in split:
        steps = jnp.exp(jax.random.uniform(jax.random.fold_in(own, position), (blocks,), jnp.float32, low / len(split), top_value / len(split)))
        factor_of = factor_of * jnp.repeat(steps, shape[position] // blocks).reshape([-1 if axis == position else 1 for axis in range(len(shape))])
    return factor_of


def centred(key, shape, scale, limit, cuts=(), kind=jnp.bfloat16):
    level = levels(key, shape, cuts, -0.22, 0.18) if cuts else 1.0
    array = jax.random.normal(key, shape, jnp.float32) * scale * level
    return jnp.minimum(jnp.maximum(array, -limit), limit).astype(kind)


def gaussian_with(key, extent, width, bound, split, heavy, dtype=jnp.bfloat16):
    entries = width * jax.random.normal(key, extent, jnp.float32)
    if split:
        entries = entries * levels(key, extent, split, -0.22, 0.18)
    return jnp.clip(spiked(entries, jax.random.fold_in(key, 3), *heavy), -bound, bound).astype(dtype)


def setup_inputs(seed: int = 0, part: int = 0) -> dict:
    key_list = jax.random.split(jax.random.key(seed), 14)
    part_keys = jax.random.split(jax.random.fold_in(key_list[13], part), 14)
    return {
        "inputs": centred(part_keys[0], (TOKENS, MODEL_WIDTH), 1.0, 6.0, ((0, 4), (1, 4))),
        "output_gradient": gaussian_with(part_keys[1], (TOKENS, MODEL_WIDTH), 1.0, 6.0, ((0, 4), (1, 4)), (1, 0, 4, 2.0)),
        "gate_preactivation": centred(part_keys[2], (TOKENS, HIDDEN_COUNT), 1.0, 6.0, ((1, 4),)),
        "up_preactivation": centred(part_keys[3], (TOKENS, HIDDEN_COUNT), 1.0, 6.0, ((1, 4),)),
        "gate_weight": centred(key_list[4], (MODEL_WIDTH, HIDDEN_COUNT), MODEL_WIDTH ** -0.5, 0.046875, ((0, 4), (1, 4))),
        "up_weight": centred(key_list[5], (MODEL_WIDTH, HIDDEN_COUNT), MODEL_WIDTH ** -0.5, 0.046875, ((0, 4), (1, 4))),
        "down_weight": centred(key_list[6], (HIDDEN_COUNT, MODEL_WIDTH), HIDDEN_COUNT ** -0.5, 0.0625, ((0, 4), (1, 4))),
        "up_adapter_entry": centred(key_list[7], (ADAPTER_RANK, MODEL_WIDTH), 1.0, 6.0, ((1, 4),)),
        "up_adapter_exit": centred(key_list[8], (ADAPTER_RANK, HIDDEN_COUNT), 0.00055, 0.0032958984, ((1, 4),)),
        "down_adapter_entry": centred(key_list[9], (ADAPTER_RANK, HIDDEN_COUNT), 1.0, 6.0, ((1, 4),)),
        "down_adapter_exit": centred(key_list[10], (ADAPTER_RANK, MODEL_WIDTH), 0.0004, 0.0023956299, ((1, 4),)),
        "up_adapter_activations": centred(part_keys[11], (ADAPTER_RANK, TOKENS), 0.05, 0.29882812),
        "down_adapter_activations": centred(part_keys[12], (ADAPTER_RANK, TOKENS), 0.05, 0.29882812),
    }


adapter_scale = 2.0


def reference(inputs, output_gradient, gate_preactivation, up_preactivation, gate_weight, up_weight, down_weight, up_adapter_entry, up_adapter_exit, down_adapter_entry, down_adapter_exit, up_adapter_activations, down_adapter_activations):
    highest_setting = lax.Precision.HIGHEST
    gate_f = gate_preactivation.astype(jnp.float32)
    up_f = up_preactivation.astype(jnp.float32)
    sig = jax.nn.sigmoid(gate_f)
    hidden_state = (gate_f * sig * up_f).astype(jnp.bfloat16)
    down_adapter_term = jnp.dot(output_gradient, down_adapter_exit.T, preferred_element_type=jnp.float32)
    hidden_gradient = jnp.dot(output_gradient, down_weight.T, preferred_element_type=jnp.float32)
    hidden_gradient = hidden_gradient + adapter_scale * jnp.dot(down_adapter_term, down_adapter_entry.astype(jnp.float32), precision=highest_setting)
    gate_grad = (hidden_gradient * up_f * sig * (1.0 + gate_f * (1.0 - sig))).astype(jnp.bfloat16)
    up_gradient = (hidden_gradient * gate_f * sig).astype(jnp.bfloat16)
    up_adapter_term = jnp.dot(up_gradient, up_adapter_exit.T, preferred_element_type=jnp.float32)
    grand_total = jnp.dot(gate_grad, gate_weight.T, preferred_element_type=jnp.float32)
    grand_total = grand_total + jnp.dot(up_gradient, up_weight.T, preferred_element_type=jnp.float32)
    grand_total = grand_total + adapter_scale * jnp.dot(up_adapter_term, up_adapter_entry.astype(jnp.float32), precision=highest_setting)
    grad_inputs = grand_total.astype(jnp.bfloat16)
    up_entry_gradient = adapter_scale * jnp.dot(up_adapter_term.T, inputs.astype(jnp.float32), precision=highest_setting)
    up_exit_gradient = adapter_scale * jnp.dot(up_adapter_activations, up_gradient, preferred_element_type=jnp.float32)
    down_rounded_value = down_adapter_term.astype(jnp.bfloat16)
    down_entry_gradient = adapter_scale * jnp.dot(down_rounded_value.T, hidden_state, preferred_element_type=jnp.float32)
    down_exit_gradient = adapter_scale * jnp.dot(down_adapter_activations, output_gradient, preferred_element_type=jnp.float32)
    return (grad_inputs, up_entry_gradient, up_exit_gradient, down_entry_gradient, down_exit_gradient)
```

```python
import functools

import jax
import jax.numpy as jnp
from jax import lax
from jax.experimental import pallas as pl
from jax.experimental.pallas import tpu as pltpu
from jax.sharding import PartitionSpec as P

adapter_scale = 2.0
HIGHEST = lax.Precision.HIGHEST
LANES = 128
VMEM_SPEC = pl.BlockSpec(memory_space=pltpu.VMEM)
ANY_SPEC = pl.BlockSpec(memory_space=pl.ANY)
f32 = jnp.float32
bf16 = jnp.bfloat16


def contract_trailing(left, right):
    return lax.dot_general(
        left, right, (((1,), (1,)), ((), ())), preferred_element_type=f32
    )


def contract_leading(left, right, matmul_accuracy=None):
    return lax.dot_general(
        left,
        right,
        (((0,), (0,)), ((), ())),
        precision=matmul_accuracy,
        preferred_element_type=f32,
    )


def in_vmem(x):
    return pltpu.with_memory_space_constraint(x, pltpu.VMEM)


def call(kernel, out_shape, *args, scratch=(), specs=None, vmem=16 << 20, cost=None):
    outs = out_shape if isinstance(out_shape, (tuple, list)) else (out_shape,)
    out_specs = tuple(VMEM_SPEC for _ in outs)
    result = pl.pallas_call(
        kernel,
        out_shape=tuple(outs),
        in_specs=specs if specs is not None else [VMEM_SPEC] * len(args),
        out_specs=out_specs,
        scratch_shapes=list(scratch),
        compiler_params=pltpu.CompilerParams(vmem_limit_bytes=vmem),
        cost_estimate=cost,
    )(*args)
    return result if isinstance(out_shape, (tuple, list)) else result[0]


def shape(dims, dtype):
    return jax.ShapeDtypeStruct(dims, dtype)


def fetch_kernel(pieces, src, dst, sems):
    rows = src.shape[0] // pieces
    copies = [
        pltpu.make_async_copy(
            src.at[pl.ds(i * rows, rows)], dst.at[pl.ds(i * rows, rows)], sems.at[i]
        )
        for i in range(pieces)
    ]
    for c in copies:
        c.start()
    for c in copies:
        c.wait()


def fetch(weight, pieces=8):
    cost = pl.CostEstimate(flops=0, transcendentals=0, bytes_accessed=2 * weight.size * 2)
    return call(
        functools.partial(fetch_kernel, pieces),
        pltpu.VMEM(weight.shape, weight.dtype),
        weight,
        scratch=[pltpu.SemaphoreType.DMA((pieces,))],
        specs=[ANY_SPEC],
        cost=cost,
    )


def factors_kernel(g_ref, u_ref, a_ref, b_ref, h_ref):
    g = g_ref[...].astype(f32)
    u = u_ref[...].astype(f32)
    q = 1.0 / (1.0 + jnp.exp(-g))
    b = g * q
    a_ref[...] = u * q * (1.0 + g * (1.0 - q))
    b_ref[...] = b
    h_ref[...] = (b * u).astype(bf16)


def split_terms(x):
    hi = x.astype(bf16)
    rest = x - hi.astype(f32)
    mid = rest.astype(bf16)
    low = (rest - mid.astype(f32)).astype(bf16)
    return hi, mid, low


def join_terms(hi, mid, low):
    return hi.astype(f32) + (mid.astype(f32) + low.astype(f32))


def store_terms(ref, start, x):
    n = x.shape[0]
    for i, term in enumerate(split_terms(x)):
        ref[start + i * n : start + (i + 1) * n, :] = term


def load_terms(ref, start, n):
    return join_terms(*(ref[start + i * n : start + (i + 1) * n, :] for i in range(3)))


def place_rows(full, pieces, position):
    n = pieces[0].shape[0]
    for k, piece in enumerate(pieces):
        full[pl.ds(pl.multiple_of((position ^ k) * n, n), n), :] = piece[...]


def hidden_kernel(flip, block, o0, o1, o2, o3, w, exit_ref, entry, out, low_ref, full):
    place_rows(full, (o0, o1, o2, o3), lax.axis_index("row"))
    half = out.shape[1]
    which = lax.rem(lax.axis_index("col"), 2) ^ flip
    low = contract_trailing(exit_ref[...], full[...])
    low_ref[...] = low
    for i in range(half // block):
        rows = pl.ds(pl.multiple_of(which * half + i * block, block), block)
        out[:, i * block : (i + 1) * block] = contract_trailing(
            full[...], w[rows, :]
        ) + adapter_scale * contract_leading(
            low, entry[:, rows].astype(f32), HIGHEST
        )


def payload_kernel(keep, got, low, low_got, out):
    total = keep[...] + got[...]
    rows, half = total.shape
    for i in range(half // LANES):
        out[i * rows : (i + 1) * rows, :] = total[:, i * LANES : (i + 1) * LANES].astype(bf16)
    store_terms(out, half // LANES * rows, low[...] + low_got[...])


def gradient_kernel(mine, other, a, b, out, low_ref):
    rows = a.shape[0]
    half = out.shape[2]
    rank = low_ref.shape[0]
    blocks = half // LANES
    start = pl.multiple_of(lax.rem(lax.axis_index("col"), 2) * half, half)
    for i in range(blocks):
        here = slice(i * rows, (i + 1) * rows)
        grad = mine[here, :].astype(f32) + other[here, :].astype(f32)
        lanes = pl.ds(pl.multiple_of(start + i * LANES, LANES), LANES)
        out[0, :, i * LANES : (i + 1) * LANES] = (grad * a[:, lanes]).astype(bf16)
        out[1, :, i * LANES : (i + 1) * LANES] = (grad * b[:, lanes]).astype(bf16)
    low_ref[...] = load_terms(mine, blocks * rows, rank) + load_terms(other, blocks * rows, rank)


def inputs_kernel(first, with_low, block, own, mate, wg, wu, exit_ref, entry, *rest):
    own_out, s1, s2, s3 = rest[:4]
    low_ref = rest[4] if with_low else None
    gg, ug, acc = rest[-3:]
    half = own.shape[2]
    width = acc.shape[1]
    rank = exit_ref.shape[0]
    par = lax.rem(lax.axis_index("col"), 2)
    mine = pl.ds(pl.multiple_of(par * half, half), half)
    theirs = pl.ds(pl.multiple_of((1 - par) * half, half), half)
    gg[:, mine] = own[0]
    ug[:, mine] = own[1]
    gg[:, theirs] = mate[0]
    ug[:, theirs] = mate[1]
    low = contract_trailing(exit_ref[...], ug[...])
    for i in range(width // block):
        rows = slice(first + i * block, first + (i + 1) * block)
        acc[:, i * block : (i + 1) * block] = (
            contract_trailing(gg[...], wg[rows, :])
            + contract_trailing(ug[...], wu[rows, :])
            + adapter_scale * contract_leading(low, entry[:, rows].astype(f32), HIGHEST)
        )
    row = lax.axis_index("row")
    n = own_out.shape[0]
    own_out[...] = acc[pl.ds(pl.multiple_of(row * n, n), n), :]
    for k, out in ((1, s1), (2, s2), (3, s3)):
        dest = pl.ds(pl.multiple_of((row ^ k) * n, n), n)
        for i in range(width // LANES):
            out[i * n : (i + 1) * n, :] = acc[dest, i * LANES : (i + 1) * LANES].astype(bf16)
        if with_low:
            store_terms(out, width // LANES * n, low)
    if with_low:
        low_ref[...] = low


def finish_kernel(own, r1, r2, r3, out):
    n, width = own.shape
    for i in range(width // LANES):
        here = slice(i * n, (i + 1) * n)
        lanes = slice(i * LANES, (i + 1) * LANES)
        out[:, lanes] = (
            own[:, lanes]
            + r1[here, :].astype(f32)
            + r2[here, :].astype(f32)
            + r3[here, :].astype(f32)
        ).astype(bf16)


def entry_kernel(offset, i0, i1, i2, i3, low, r1, r2, r3, out, full, lows):
    row = lax.axis_index("row")
    rank = low.shape[0]
    place_rows(full, (i0, i1, i2, i3), row)
    lows[row] = low[...]
    for k, ref in ((1, r1), (2, r2), (3, r3)):
        lows[row ^ k] = load_terms(ref, offset, rank)
    total = (lows[0] + lows[1]) + (lows[2] + lows[3])
    parts = split_terms(total)
    full_inputs = full[...]
    out[...] = adapter_scale * sum(
        jnp.dot(part, full_inputs, preferred_element_type=f32) for part in parts
    )


def small_kernel(own, mate, low, hidden, up_act, down_act, o0, o1, o2, o3, up_exit, down_entry, down_exit, full, ug):
    half = own.shape[2]
    par = lax.rem(lax.axis_index("col"), 2)
    ug[:, pl.ds(pl.multiple_of(par * half, half), half)] = own[1]
    ug[:, pl.ds(pl.multiple_of((1 - par) * half, half), half)] = mate[1]
    place_rows(full, (o0, o1, o2, o3), lax.axis_index("row"))
    up_exit[...] = adapter_scale * jnp.dot(up_act[...], ug[...], preferred_element_type=f32)
    down_entry[...] = adapter_scale * jnp.dot(
        low[...].astype(bf16), hidden[...], preferred_element_type=f32
    )
    down_exit[...] = adapter_scale * jnp.dot(down_act[...], full[...], preferred_element_type=f32)


def swap(x, axis, distance, n):
    return lax.ppermute(x, axis, [(i, i ^ distance) for i in range(n)])


CHUNKS = 2


def exchange_body(
    inputs,
    output_gradient,
    gate_preactivation,
    up_preactivation,
    gate_weight,
    up_weight,
    down_weight,
    up_adapter_entry,
    up_adapter_exit,
    down_adapter_entry,
    down_adapter_exit,
    up_adapter_activations,
    down_adapter_activations,
):
    tokens, hidden = gate_preactivation.shape
    share, width = output_gradient.shape
    rank = up_adapter_exit.shape[0]
    half = hidden // 2
    own_gradient = output_gradient
    gathered = [swap(own_gradient, "row", k, 4) for k in (1, 2, 3)]
    down_v = fetch(down_weight)
    gate_v = fetch(gate_weight)
    up_v = fetch(up_weight)
    a, b, hidden_state = call(
        factors_kernel,
        (shape((tokens, hidden), f32), shape((tokens, hidden), f32), shape((tokens, hidden), bf16)),
        gate_preactivation,
        up_preactivation,
    )
    gathered_inputs = [swap(inputs, "row", k, 4) for k in (1, 2, 3)]

    def hidden_half(flip):
        return call(
            functools.partial(hidden_kernel, flip, 512),
            (shape((tokens, half), f32), shape((rank, tokens), f32)),
            own_gradient,
            *gathered,
            in_vmem(down_v),
            down_adapter_exit,
            down_adapter_entry,
            scratch=[pltpu.VMEM((tokens, width), bf16)],
        )

    send, low_piece = hidden_half(1)
    got = swap(send, "col", 1, 4)
    low_got = swap(low_piece, "col", 1, 4)
    keep, low_piece2 = hidden_half(0)
    blocks = half // LANES
    payload = call(
        payload_kernel,
        shape((blocks * tokens + 3 * rank, LANES), bf16),
        keep,
        got,
        low_piece2,
        low_got,
    )
    other = swap(payload, "col", 2, 4)
    grads, low_full = call(
        gradient_kernel,
        (shape((2, tokens, half), bf16), shape((rank, tokens), f32)),
        payload,
        other,
        a,
        b,
    )
    mate_grads = swap(grads, "col", 1, 4)

    part = width // CHUNKS
    rows = part // LANES * share
    owns, received = [], []
    low_up = None
    for c in range(CHUNKS):
        with_low = c == 0
        sent = shape((rows + (3 * rank if with_low else 0), LANES), bf16)
        outs = call(
            functools.partial(inputs_kernel, c * part, with_low, 512),
            (shape((share, part), f32), sent, sent, sent)
            + ((shape((rank, tokens), f32),) if with_low else ()),
            grads,
            mate_grads,
            in_vmem(gate_v),
            in_vmem(up_v),
            up_adapter_exit,
            up_adapter_entry,
            scratch=[
                pltpu.VMEM((tokens, hidden), bf16),
                pltpu.VMEM((tokens, hidden), bf16),
                pltpu.VMEM((tokens, part), f32),
            ],
        )
        if with_low:
            low_up = outs[4]
        owns.append(outs[0])
        received.append([swap(outs[k], "row", k, 4) for k in (1, 2, 3)])
    up_exit_gradient, down_entry_gradient, down_exit_gradient = call(
        small_kernel,
        (shape((rank, hidden), f32), shape((rank, hidden), f32), shape((rank, width), f32)),
        grads,
        mate_grads,
        low_full,
        hidden_state,
        up_adapter_activations,
        down_adapter_activations,
        own_gradient,
        *gathered,
        scratch=[pltpu.VMEM((tokens, width), bf16), pltpu.VMEM((tokens, hidden), bf16)],
    )
    up_entry_gradient = call(
        functools.partial(entry_kernel, rows),
        shape((rank, width), f32),
        inputs,
        *gathered_inputs,
        low_up,
        *received[0],
        scratch=[pltpu.VMEM((tokens, width), bf16), pltpu.VMEM((4, rank, tokens), f32)],
    )
    pieces = [
        call(finish_kernel, shape((share, part), bf16), owns[c], *received[c])
        for c in range(CHUNKS)
    ]
    return (
        jnp.concatenate(pieces, axis=1),
        up_entry_gradient,
        up_exit_gradient,
        down_entry_gradient,
        down_exit_gradient,
    )


def body(
    inputs,
    output_gradient,
    gate_preactivation,
    up_preactivation,
    gate_weight,
    up_weight,
    down_weight,
    up_adapter_entry,
    up_adapter_exit,
    down_adapter_entry,
    down_adapter_exit,
    up_adapter_activations,
    down_adapter_activations,
):
    highest_setting = HIGHEST
    complete_gradient = lax.all_gather(output_gradient, "row", axis=0, tiled=True)
    down_piece = contract_trailing(complete_gradient, down_adapter_exit)
    hidden_piece = contract_trailing(complete_gradient, down_weight)
    hidden_piece = hidden_piece + adapter_scale * jnp.dot(
        down_piece, down_adapter_entry.astype(f32), precision=highest_setting
    )
    hidden_gradient, down_full = lax.psum((hidden_piece, down_piece), "col")
    gate_f = gate_preactivation.astype(f32)
    up_f = up_preactivation.astype(f32)
    sigmoid_gate = jax.nn.sigmoid(gate_f)
    hidden_state = (gate_f * sigmoid_gate * up_f).astype(bf16)
    gate_grad = (
        hidden_gradient * up_f * sigmoid_gate * (1.0 + gate_f * (1.0 - sigmoid_gate))
    ).astype(bf16)
    up_gradient = (hidden_gradient * gate_f * sigmoid_gate).astype(bf16)
    down_rounded_value = down_full.astype(bf16)
    upper_piece = contract_trailing(up_gradient, up_adapter_exit)
    input_piece = contract_trailing(gate_grad, gate_weight) + contract_trailing(
        up_gradient, up_weight
    )
    input_piece = input_piece + adapter_scale * jnp.dot(
        upper_piece, up_adapter_entry.astype(f32), precision=highest_setting
    )
    input_grad, upper_full = (
        lax.psum_scatter(input_piece, "row", scatter_dimension=0, tiled=True),
        lax.psum_scatter(upper_piece, "row", scatter_dimension=0, tiled=True),
    )
    up_entry_term = adapter_scale * contract_leading(
        upper_full, inputs.astype(f32), matmul_accuracy=highest_setting
    )
    up_entry_gradient = lax.psum(up_entry_term, "row")
    up_exit_gradient = adapter_scale * jnp.dot(
        up_adapter_activations, up_gradient, preferred_element_type=f32
    )
    down_entry_gradient = adapter_scale * contract_leading(down_rounded_value, hidden_state)
    down_exit_gradient = adapter_scale * jnp.dot(
        down_adapter_activations, complete_gradient, preferred_element_type=f32
    )
    return (
        input_grad.astype(bf16),
        up_entry_gradient,
        up_exit_gradient,
        down_entry_gradient,
        down_exit_gradient,
    )


def solution(mesh):
    placed = (
        P(("grp", "row"), "col"),
        P(("grp", "row"), "col"),
        P("grp", "row"),
        P("grp", "row"),
        P("col", "row"),
        P("col", "row"),
        P("row", "col"),
        P(None, "col"),
        P(None, "row"),
        P(None, "row"),
        P(None, "col"),
        P(None, "grp"),
        P(None, "grp"),
    )
    exchange = mesh.shape["row"] == 4 and mesh.shape["col"] == 4
    return jax.shard_map(
        exchange_body if exchange else body,
        mesh=mesh,
        in_specs=placed,
        out_specs=(
            P(("grp", "row"), "col"),
            P("grp", "col"),
            P("grp", "row"),
            P("grp", "row"),
            P("grp", "col"),
        ),
        check_vma=False,
    )
```

```python
import functools

import jax
import jax.numpy as jnp
from jax import lax
from jax.experimental import pallas as pl
from jax.experimental.pallas import tpu as pltpu
from jax.sharding import PartitionSpec as P

adapter_scale = 2.0
HIGHEST = lax.Precision.HIGHEST
LANES = 128
VMEM_SPEC = pl.BlockSpec(memory_space=pltpu.VMEM)
HBM_SPEC = pl.BlockSpec(memory_space=pltpu.HBM)
f32 = jnp.float32
bf16 = jnp.bfloat16


def contract_trailing(left, right):
    return lax.dot_general(
        left, right, (((1,), (1,)), ((), ())), preferred_element_type=f32
    )


def contract_leading(left, right, matmul_accuracy=None):
    return lax.dot_general(
        left,
        right,
        (((0,), (0,)), ((), ())),
        precision=matmul_accuracy,
        preferred_element_type=f32,
    )


def in_vmem(x):
    return pltpu.with_memory_space_constraint(x, pltpu.VMEM)


def after(x, *others):
    return lax.optimization_barrier((x, *others))[0]


def call(kernel, out_shape, *args, scratch=(), specs=None, vmem=7 << 20):
    outs = out_shape if isinstance(out_shape, (tuple, list)) else (out_shape,)
    out_specs = tuple(VMEM_SPEC for _ in outs)
    result = pl.pallas_call(
        kernel,
        out_shape=tuple(outs),
        in_specs=specs if specs is not None else [VMEM_SPEC] * len(args),
        out_specs=out_specs,
        scratch_shapes=list(scratch),
        compiler_params=pltpu.CompilerParams(vmem_limit_bytes=vmem),
        cost_estimate=pl.CostEstimate(flops=0, transcendentals=0, bytes_accessed=0),
    )(*args)
    return result if isinstance(out_shape, (tuple, list)) else result[0]


def shape(dims, dtype):
    return jax.ShapeDtypeStruct(dims, dtype)


def fetch_kernel(pieces, first, src, dst, sems):
    rows = dst.shape[0] // pieces
    copies = [
        pltpu.make_async_copy(
            src.at[pl.ds(first + i * rows, rows)],
            dst.at[pl.ds(i * rows, rows)],
            sems.at[i],
        )
        for i in range(pieces)
    ]
    for c in copies:
        c.start()
    for c in copies:
        c.wait()


def fetch(weight, first, rows, pieces=4):
    return call(
        functools.partial(fetch_kernel, pieces, first),
        pltpu.VMEM((rows, weight.shape[1]), weight.dtype),
        pltpu.with_memory_space_constraint(weight, pltpu.HBM),
        scratch=[pltpu.SemaphoreType.DMA((pieces,))],
        specs=[HBM_SPEC],
        vmem=1 << 20,
    )


def factors_kernel(g_ref, u_ref, a_ref, b_ref, h_ref):
    g = g_ref[...].astype(f32)
    u = u_ref[...].astype(f32)
    q = 1.0 / (1.0 + jnp.exp(-g))
    b = g * q
    a_ref[...] = u * q * (1.0 + g * (1.0 - q))
    b_ref[...] = b
    h_ref[...] = (b * u).astype(bf16)


def split_terms(x):
    hi = x.astype(bf16)
    rest = x - hi.astype(f32)
    mid = rest.astype(bf16)
    low = (rest - mid.astype(f32)).astype(bf16)
    return hi, mid, low


def join_terms(hi, mid, low):
    return hi.astype(f32) + (mid.astype(f32) + low.astype(f32))


def store_terms(ref, start, x):
    n = x.shape[0]
    for i, term in enumerate(split_terms(x)):
        ref[start + i * n : start + (i + 1) * n, :] = term


def load_terms(ref, start, n):
    return join_terms(*(ref[start + i * n : start + (i + 1) * n, :] for i in range(3)))


def place_rows(full, pieces, position):
    n = pieces[0].shape[0]
    for k, piece in enumerate(pieces):
        full[pl.ds(pl.multiple_of((position ^ k) * n, n), n), :] = piece[...]


def hidden_kernel(flip, half, block, o0, o1, o2, o3, w, exit_ref, entry, *rest):
    outs, full = rest[:-1], rest[-1]
    n = outs[0].shape[0]
    place_rows(full, (o0, o1, o2, o3), lax.axis_index("row"))
    which = lax.rem(lax.axis_index("col"), 2) ^ flip
    low = contract_trailing(exit_ref[...], full[...])
    outs[0][: low.shape[0], half:] = low
    for i in range(half // block):
        rows = pl.ds(pl.multiple_of(which * half + i * block, block), block)
        piece = contract_trailing(full[...], w[rows, :]) + adapter_scale * contract_leading(
            low, entry[:, rows].astype(f32), HIGHEST
        )
        for j, out in enumerate(outs):
            out[:, i * block : (i + 1) * block] = piece[j * n : (j + 1) * n, :]


def payload_kernel(rank, half, keep, *rest):
    got, outs = rest[:-2], rest[-2:]
    rows = keep.shape[0]
    n = got[0].shape[0]
    blocks = half // LANES // 2
    for j, ref in enumerate(got):
        total = keep[j * n : (j + 1) * n, :] + ref[...]
        for i in range(2 * blocks):
            first = i % blocks * rows + j * n
            outs[i // blocks][first : first + n, :] = total[
                :, i * LANES : (i + 1) * LANES
            ].astype(bf16)
        if j == 0:
            store_terms(outs[0], blocks * rows, total[:rank, half:])


def gradient_kernel(mine0, mine1, other0, other1, a, b, *outs):
    gate_outs, up_outs, low_ref = outs[:2], outs[2:4], outs[4]
    rows = a.shape[0]
    n, half = up_outs[0].shape
    rank = low_ref.shape[0]
    blocks = half // LANES // 2
    start = pl.multiple_of(lax.rem(lax.axis_index("col"), 2) * half, half)
    for i in range(2 * blocks):
        here = slice(i % blocks * rows, (i % blocks + 1) * rows)
        mine, other = (mine0, other0) if i < blocks else (mine1, other1)
        grad = mine[here, :].astype(f32) + other[here, :].astype(f32)
        lanes = pl.ds(pl.multiple_of(start + i * LANES, LANES), LANES)
        for refs, factor in ((gate_outs, a), (up_outs, b)):
            value = (grad * factor[:, lanes]).astype(bf16)
            for j, ref in enumerate(refs):
                ref[:, i * LANES : (i + 1) * LANES] = value[j * n : (j + 1) * n, :]
    low_ref[...] = load_terms(mine0, blocks * rows, rank) + load_terms(other0, blocks * rows, rank)


def place_halves(full, own, mate):
    n, half = own[0].shape
    par = lax.rem(lax.axis_index("col"), 2)
    for position, refs in ((par, own), (1 - par, mate)):
        lanes = pl.ds(pl.multiple_of(position * half, half), half)
        for j, ref in enumerate(refs):
            full[j * n : (j + 1) * n, lanes] = ref[...]


def inputs_kernel(first, with_low, block, *refs):
    own, mate, (wg, wu, exit_ref, entry), rest = refs[:4], refs[4:8], refs[8:12], refs[12:]
    own_out, s1, s2, s3 = rest[:4]
    low_ref = rest[4] if with_low else None
    gg, ug, acc = rest[-3:]
    width = acc.shape[1]
    rank = exit_ref.shape[0]
    place_halves(gg, own[:2], mate[:2])
    place_halves(ug, own[2:], mate[2:])
    low = contract_trailing(exit_ref[...], ug[...])
    for i in range(width // block):
        rows = slice(i * block, (i + 1) * block)
        lanes = slice(first + i * block, first + (i + 1) * block)
        acc[:, i * block : (i + 1) * block] = (
            contract_trailing(gg[...], wg[rows, :])
            + contract_trailing(ug[...], wu[rows, :])
            + adapter_scale * contract_leading(low, entry[:, lanes].astype(f32), HIGHEST)
        )
    row = lax.axis_index("row")
    n = own_out.shape[0]
    own_out[...] = acc[pl.ds(pl.multiple_of(row * n, n), n), :]
    for k, out in ((1, s1), (2, s2), (3, s3)):
        dest = pl.ds(pl.multiple_of((row ^ k) * n, n), n)
        for i in range(width // LANES):
            out[i * n : (i + 1) * n, :] = acc[dest, i * LANES : (i + 1) * LANES].astype(bf16)
        if with_low:
            store_terms(out, width // LANES * n, low)
    if with_low:
        low_ref[...] = low


def finish_kernel(own, r1, r2, r3, *rest):
    done, out = rest[:-1], rest[-1]
    n, width = own.shape
    first = out.shape[1] - width
    for ref in done:
        out[:, :first] = ref[...]
    for i in range(width // LANES):
        here = slice(i * n, (i + 1) * n)
        lanes = slice(i * LANES, (i + 1) * LANES)
        out[:, first + i * LANES : first + (i + 1) * LANES] = (
            own[:, lanes]
            + r1[here, :].astype(f32)
            + r2[here, :].astype(f32)
            + r3[here, :].astype(f32)
        ).astype(bf16)


def stack_kernel(top, bottom, *outs):
    n = top.shape[0]
    first = 0
    for out in outs:
        lanes = slice(first, first + out.shape[1])
        out[:n, :] = top[:, lanes]
        out[n:, :] = bottom[:, lanes]
        first = lanes.stop


def entry_kernel(offset, pieces, low, r1, r2, r3, *rest):
    near, far = rest[:pieces], rest[pieces : 2 * pieces]
    out, full, lows = rest[2 * pieces :]
    row = lax.axis_index("row")
    rank = low.shape[0]
    n = near[0].shape[0] // 2
    first = 0
    for here, there in zip(near, far):
        lanes = slice(first, first + here.shape[1])
        for k in range(4):
            ref = here if k < 2 else there
            rows = pl.ds(pl.multiple_of((row ^ k) * n, n), n)
            full[rows, lanes] = ref[(k % 2) * n : (k % 2 + 1) * n, :]
        first = lanes.stop
    lows[row] = low[...]
    for k, ref in ((1, r1), (2, r2), (3, r3)):
        lows[row ^ k] = load_terms(ref, offset, rank)
    total = (lows[0] + lows[1]) + (lows[2] + lows[3])
    whole = full[...]
    out[...] = adapter_scale * sum(
        jnp.dot(term, whole, preferred_element_type=f32) for term in split_terms(total)
    )


def small_kernel(
    own0, own1, mate0, mate1, low, hidden, up_act, down_act, o0, o1, o2, o3, *rest
):
    up_exit, down_entry, down_exit, full, ug = rest
    place_halves(ug, (own0, own1), (mate0, mate1))
    place_rows(full, (o0, o1, o2, o3), lax.axis_index("row"))
    up_exit[...] = adapter_scale * jnp.dot(up_act[...], ug[...], preferred_element_type=f32)
    down_entry[...] = adapter_scale * jnp.dot(
        low[...].astype(bf16), hidden[...], preferred_element_type=f32
    )
    down_exit[...] = adapter_scale * jnp.dot(down_act[...], full[...], preferred_element_type=f32)


def swap(x, axis, distance, n):
    return lax.ppermute(x, axis, [(i, i ^ distance) for i in range(n)])


EIGHTHS = (4,4)
CHUNKS = len(EIGHTHS)


def exchange_body(
    inputs,
    output_gradient,
    gate_preactivation,
    up_preactivation,
    gate_weight,
    up_weight,
    down_weight,
    up_adapter_entry,
    up_adapter_exit,
    down_adapter_entry,
    down_adapter_exit,
    up_adapter_activations,
    down_adapter_activations,
):
    tokens, hidden = gate_preactivation.shape
    share, width = output_gradient.shape
    rank = up_adapter_exit.shape[0]
    half = hidden // 2
    own_gradient = output_gradient
    gathered = [swap(own_gradient, "row", k, 4) for k in (1, 2, 3)]
    parts = [width // 8 * e for e in EIGHTHS]
    firsts = [sum(parts[:c]) for c in range(CHUNKS)]
    down_v = fetch(down_weight, 0, hidden)
    gate_v = [fetch(gate_weight, firsts[c], parts[c]) for c in range(CHUNKS)]
    up_v = [fetch(up_weight, firsts[c], parts[c]) for c in range(CHUNKS)]
    a, b, hidden_state = call(
        factors_kernel,
        (shape((tokens, hidden), f32), shape((tokens, hidden), f32), shape((tokens, hidden), bf16)),
        gate_preactivation,
        up_preactivation,
    )
    near = [call(stack_kernel, shape((2 * share, width), bf16), inputs, swap(inputs, "row", 1, 4))]
    down_v = after(down_v, gate_v, up_v, a, b, near)

    def hidden_half(flip, gradient, split):
        return call(
            functools.partial(hidden_kernel, flip, half, 512),
            (shape((tokens // split, half + LANES), f32),) * split,
            gradient,
            *gathered,
            in_vmem(down_v),
            down_adapter_exit,
            down_adapter_entry,
            scratch=[pltpu.VMEM((tokens, width), bf16)],
        )

    send = hidden_half(1, own_gradient, 4)
    got = [swap(x, "col", 1, 4) for x in send]
    keep = hidden_half(0, after(own_gradient, send), 1)[0]
    blocks = half // LANES
    far = [swap(near[0], "row", 2, 4)]
    payload = call(
        functools.partial(payload_kernel, rank, half),
        (
            shape((blocks // 2 * tokens + 3 * rank, LANES), bf16),
            shape((blocks // 2 * tokens, LANES), bf16),
        ),
        keep,
        *got,
    )
    other = [swap(x, "col", 2, 4) for x in payload]
    *grads, low_full = call(
        gradient_kernel,
        (shape((tokens // 2, half), bf16),) * 4 + (shape((rank, tokens), f32),),
        *payload,
        *other,
        a,
        b,
    )
    mate_grads = [swap(x, "col", 1, 4) for x in grads]

    owns, received = [], []
    outs = ()
    for c in range(CHUNKS):
        with_low = c == 0
        rows = parts[c] // LANES * share
        sent = shape((rows + (3 * rank if with_low else 0), LANES), bf16)
        outs = call(
            functools.partial(inputs_kernel, firsts[c], with_low, 512),
            (shape((share, parts[c]), f32), sent, sent, sent)
            + ((shape((rank, tokens), f32),) if with_low else ()),
            *grads,
            *mate_grads,
            in_vmem(after(gate_v[c], outs, far) if c else gate_v[c]),
            in_vmem(up_v[c]),
            up_adapter_exit,
            up_adapter_entry,
            scratch=[
                pltpu.VMEM((tokens, hidden), bf16),
                pltpu.VMEM((tokens, hidden), bf16),
                pltpu.VMEM((tokens, parts[c]), f32),
            ],
        )
        if with_low:
            low_up = outs[4]
        owns.append(outs[0])
        received.append([swap(outs[k], "row", k, 4) for k in (1, 2, 3)])
    input_grad = ()
    for c in range(CHUNKS):
        done = shape((share, firsts[c] + parts[c]), bf16)
        own = after(owns[c], owns[c + 1]) if c + 1 < CHUNKS else owns[c]
        input_grad = (call(finish_kernel, done, own, *received[c], *input_grad),)
    entry_sum = call(
        functools.partial(entry_kernel, parts[0] // LANES * share, 1),
        shape((rank, width), f32),
        after(low_up, owns),
        *received[0],
        *near,
        *far,
        scratch=[pltpu.VMEM((tokens, width), bf16), pltpu.VMEM((4, rank, tokens), f32)],
    )
    up_exit_gradient, down_entry_gradient, down_exit_gradient = call(
        small_kernel,
        (shape((rank, hidden), f32), shape((rank, hidden), f32), shape((rank, width), f32)),
        *grads[2:],
        *mate_grads[2:],
        low_full,
        hidden_state,
        up_adapter_activations,
        down_adapter_activations,
        own_gradient,
        *gathered,
        scratch=[pltpu.VMEM((tokens, width), bf16), pltpu.VMEM((tokens, hidden), bf16)],
    )
    return (
        input_grad[0],
        entry_sum,
        up_exit_gradient,
        down_entry_gradient,
        down_exit_gradient,
    )


def body(
    inputs,
    output_gradient,
    gate_preactivation,
    up_preactivation,
    gate_weight,
    up_weight,
    down_weight,
    up_adapter_entry,
    up_adapter_exit,
    down_adapter_entry,
    down_adapter_exit,
    up_adapter_activations,
    down_adapter_activations,
):
    highest_setting = HIGHEST
    complete_gradient = lax.all_gather(output_gradient, "row", axis=0, tiled=True)
    down_piece = contract_trailing(complete_gradient, down_adapter_exit)
    hidden_piece = contract_trailing(complete_gradient, down_weight)
    hidden_piece = hidden_piece + adapter_scale * jnp.dot(
        down_piece, down_adapter_entry.astype(f32), precision=highest_setting
    )
    hidden_gradient, down_full = lax.psum((hidden_piece, down_piece), "col")
    gate_f = gate_preactivation.astype(f32)
    up_f = up_preactivation.astype(f32)
    sigmoid_gate = jax.nn.sigmoid(gate_f)
    hidden_state = (gate_f * sigmoid_gate * up_f).astype(bf16)
    gate_grad = (
        hidden_gradient * up_f * sigmoid_gate * (1.0 + gate_f * (1.0 - sigmoid_gate))
    ).astype(bf16)
    up_gradient = (hidden_gradient * gate_f * sigmoid_gate).astype(bf16)
    down_rounded_value = down_full.astype(bf16)
    upper_piece = contract_trailing(up_gradient, up_adapter_exit)
    input_piece = contract_trailing(gate_grad, gate_weight) + contract_trailing(
        up_gradient, up_weight
    )
    input_piece = input_piece + adapter_scale * jnp.dot(
        upper_piece, up_adapter_entry.astype(f32), precision=highest_setting
    )
    input_grad, upper_full = (
        lax.psum_scatter(input_piece, "row", scatter_dimension=0, tiled=True),
        lax.psum_scatter(upper_piece, "row", scatter_dimension=0, tiled=True),
    )
    up_entry_term = adapter_scale * contract_leading(
        upper_full, inputs.astype(f32), matmul_accuracy=highest_setting
    )
    up_entry_gradient = lax.psum(up_entry_term, "row")
    up_exit_gradient = adapter_scale * jnp.dot(
        up_adapter_activations, up_gradient, preferred_element_type=f32
    )
    down_entry_gradient = adapter_scale * contract_leading(down_rounded_value, hidden_state)
    down_exit_gradient = adapter_scale * jnp.dot(
        down_adapter_activations, complete_gradient, preferred_element_type=f32
    )
    return (
        input_grad.astype(bf16),
        up_entry_gradient,
        up_exit_gradient,
        down_entry_gradient,
        down_exit_gradient,
    )


def solution(mesh):
    placed = (
        P(("grp", "row"), "col"),
        P(("grp", "row"), "col"),
        P("grp", "row"),
        P("grp", "row"),
        P("col", "row"),
        P("col", "row"),
        P("row", "col"),
        P(None, "col"),
        P(None, "row"),
        P(None, "row"),
        P(None, "col"),
        P(None, "grp"),
        P(None, "grp"),
    )
    exchange = mesh.shape["row"] == 4 and mesh.shape["col"] == 4
    return jax.shard_map(
        exchange_body if exchange else body,
        mesh=mesh,
        in_specs=placed,
        out_specs=(
            P(("grp", "row"), "col"),
            P("grp", "col"),
            P("grp", "row"),
            P("grp", "row"),
            P("grp", "col"),
        ),
        check_vma=False,
    )
```

```python
import functools

import jax
import jax.numpy as jnp
from jax import lax
from jax.experimental import pallas as pl
from jax.experimental.pallas import tpu as pltpu
from jax.sharding import PartitionSpec as P

adapter_scale = 2.0
HIGHEST = lax.Precision.HIGHEST
LANES = 128
VMEM_SPEC = pl.BlockSpec(memory_space=pltpu.VMEM)
HBM_SPEC = pl.BlockSpec(memory_space=pltpu.HBM)
f32 = jnp.float32
bf16 = jnp.bfloat16


def contract_trailing(left, right):
    return lax.dot_general(
        left, right, (((1,), (1,)), ((), ())), preferred_element_type=f32
    )


def contract_leading(left, right, matmul_accuracy=None):
    return lax.dot_general(
        left,
        right,
        (((0,), (0,)), ((), ())),
        precision=matmul_accuracy,
        preferred_element_type=f32,
    )


def in_vmem(x):
    return pltpu.with_memory_space_constraint(x, pltpu.VMEM)


def after(x, *others):
    return lax.optimization_barrier((x, *others))[0]


def call(kernel, out_shape, *args, scratch=(), specs=None, vmem=6 << 20):
    outs = out_shape if isinstance(out_shape, (tuple, list)) else (out_shape,)
    out_specs = tuple(VMEM_SPEC for _ in outs)
    result = pl.pallas_call(
        kernel,
        out_shape=tuple(outs),
        in_specs=specs if specs is not None else [VMEM_SPEC] * len(args),
        out_specs=out_specs,
        scratch_shapes=list(scratch),
        compiler_params=pltpu.CompilerParams(vmem_limit_bytes=vmem),
        cost_estimate=pl.CostEstimate(flops=0, transcendentals=0, bytes_accessed=0),
    )(*args)
    return result if isinstance(out_shape, (tuple, list)) else result[0]


def shape(dims, dtype):
    return jax.ShapeDtypeStruct(dims, dtype)


def fetch_kernel(pieces, first, src, dst, sems):
    rows = dst.shape[0] // pieces
    copies = [
        pltpu.make_async_copy(
            src.at[pl.ds(first + i * rows, rows)],
            dst.at[pl.ds(i * rows, rows)],
            sems.at[i],
        )
        for i in range(pieces)
    ]
    for c in copies:
        c.start()
    for c in copies:
        c.wait()


def fetch(weight, first, rows, pieces=4):
    return call(
        functools.partial(fetch_kernel, pieces, first),
        pltpu.VMEM((rows, weight.shape[1]), weight.dtype),
        pltpu.with_memory_space_constraint(weight, pltpu.HBM),
        scratch=[pltpu.SemaphoreType.DMA((pieces,))],
        specs=[HBM_SPEC],
        vmem=1 << 20,
    )


def factors_kernel(g_ref, u_ref, a_ref, b_ref, h_ref):
    g = g_ref[...].astype(f32)
    u = u_ref[...].astype(f32)
    q = 1.0 / (1.0 + jnp.exp(-g))
    b = g * q
    a_ref[...] = u * q * (1.0 + g * (1.0 - q))
    b_ref[...] = b
    h_ref[...] = (b * u).astype(bf16)


def split_terms(x):
    hi = x.astype(bf16)
    rest = x - hi.astype(f32)
    mid = rest.astype(bf16)
    low = (rest - mid.astype(f32)).astype(bf16)
    return hi, mid, low


def join_terms(hi, mid, low):
    return hi.astype(f32) + (mid.astype(f32) + low.astype(f32))


def store_terms(ref, start, x):
    n = x.shape[0]
    for i, term in enumerate(split_terms(x)):
        ref[start + i * n : start + (i + 1) * n, :] = term


def load_terms(ref, start, n):
    return join_terms(*(ref[start + i * n : start + (i + 1) * n, :] for i in range(3)))


def place_rows(full, pieces, position):
    n = pieces[0].shape[0]
    for k, piece in enumerate(pieces):
        full[pl.ds(pl.multiple_of((position ^ k) * n, n), n), :] = piece[...]


def hidden_kernel(flip, half, block, o0, o1, o2, o3, w, exit_ref, entry, *rest):
    outs, full = rest[:-1], rest[-1]
    n = outs[0].shape[0]
    place_rows(full, (o0, o1, o2, o3), lax.axis_index("row"))
    which = lax.rem(lax.axis_index("col"), 2) ^ flip
    low = contract_trailing(exit_ref[...], full[...])
    outs[0][: low.shape[0], half:] = low
    for i in range(half // block):
        rows = pl.ds(pl.multiple_of(which * half + i * block, block), block)
        piece = contract_trailing(full[...], w[rows, :]) + adapter_scale * contract_leading(
            low, entry[:, rows].astype(f32), HIGHEST
        )
        for j, out in enumerate(outs):
            out[:, i * block : (i + 1) * block] = piece[j * n : (j + 1) * n, :]


def payload_kernel(rank, half, keep, *rest):
    got, outs = rest[:-2], rest[-2:]
    rows = keep.shape[0]
    n = got[0].shape[0]
    blocks = half // LANES // 2
    for j, ref in enumerate(got):
        total = keep[j * n : (j + 1) * n, :] + ref[...]
        for i in range(2 * blocks):
            first = i % blocks * rows + j * n
            outs[i // blocks][first : first + n, :] = total[
                :, i * LANES : (i + 1) * LANES
            ].astype(bf16)
        if j == 0:
            store_terms(outs[0], blocks * rows, total[:rank, half:])


def gradient_kernel(mine0, mine1, other0, other1, a, b, *outs):
    gate_outs, up_outs, low_ref = outs[:2], outs[2:4], outs[4]
    rows = a.shape[0]
    n, half = up_outs[0].shape
    rank = low_ref.shape[0]
    blocks = half // LANES // 2
    start = pl.multiple_of(lax.rem(lax.axis_index("col"), 2) * half, half)
    for i in range(2 * blocks):
        here = slice(i % blocks * rows, (i % blocks + 1) * rows)
        mine, other = (mine0, other0) if i < blocks else (mine1, other1)
        grad = mine[here, :].astype(f32) + other[here, :].astype(f32)
        lanes = pl.ds(pl.multiple_of(start + i * LANES, LANES), LANES)
        for refs, factor in ((gate_outs, a), (up_outs, b)):
            value = (grad * factor[:, lanes]).astype(bf16)
            for j, ref in enumerate(refs):
                ref[:, i * LANES : (i + 1) * LANES] = value[j * n : (j + 1) * n, :]
    low_ref[...] = load_terms(mine0, blocks * rows, rank) + load_terms(other0, blocks * rows, rank)


def place_halves(full, own, mate):
    n, half = own[0].shape
    par = lax.rem(lax.axis_index("col"), 2)
    for position, refs in ((par, own), (1 - par, mate)):
        lanes = pl.ds(pl.multiple_of(position * half, half), half)
        for j, ref in enumerate(refs):
            full[j * n : (j + 1) * n, lanes] = ref[...]


def inputs_kernel(first, with_low, block, *refs):
    own, mate, (wg, wu, exit_ref, entry), rest = refs[:4], refs[4:8], refs[8:12], refs[12:]
    own_out, s1, s2, s3 = rest[:4]
    low_ref = rest[4] if with_low else None
    gg, ug, acc = rest[-3:]
    width = acc.shape[1]
    rank = exit_ref.shape[0]
    place_halves(gg, own[:2], mate[:2])
    place_halves(ug, own[2:], mate[2:])
    low = contract_trailing(exit_ref[...], ug[...])
    for i in range(width // block):
        rows = slice(i * block, (i + 1) * block)
        lanes = slice(first + i * block, first + (i + 1) * block)
        acc[:, i * block : (i + 1) * block] = (
            contract_trailing(gg[...], wg[rows, :])
            + contract_trailing(ug[...], wu[rows, :])
            + adapter_scale * contract_leading(low, entry[:, lanes].astype(f32), HIGHEST)
        )
    row = lax.axis_index("row")
    n = own_out.shape[0]
    own_out[...] = acc[pl.ds(pl.multiple_of(row * n, n), n), :]
    for k, out in ((1, s1), (2, s2), (3, s3)):
        dest = pl.ds(pl.multiple_of((row ^ k) * n, n), n)
        for i in range(width // LANES):
            out[i * n : (i + 1) * n, :] = acc[dest, i * LANES : (i + 1) * LANES].astype(bf16)
        if with_low:
            store_terms(out, width // LANES * n, low)
    if with_low:
        low_ref[...] = low


def finish_kernel(own, r1, r2, r3, *rest):
    done, out = rest[:-1], rest[-1]
    n, width = own.shape
    first = out.shape[1] - width
    for ref in done:
        out[:, :first] = ref[...]
    for i in range(width // LANES):
        here = slice(i * n, (i + 1) * n)
        lanes = slice(i * LANES, (i + 1) * LANES)
        out[:, first + i * LANES : first + (i + 1) * LANES] = (
            own[:, lanes]
            + r1[here, :].astype(f32)
            + r2[here, :].astype(f32)
            + r3[here, :].astype(f32)
        ).astype(bf16)


def stack_kernel(top, bottom, *outs):
    n = top.shape[0]
    first = 0
    for out in outs:
        lanes = slice(first, first + out.shape[1])
        out[:n, :] = top[:, lanes]
        out[n:, :] = bottom[:, lanes]
        first = lanes.stop


def entry_kernel(offset, pieces, low, r1, r2, r3, *rest):
    near, far = rest[:pieces], rest[pieces : 2 * pieces]
    out, full, lows = rest[2 * pieces :]
    row = lax.axis_index("row")
    rank = low.shape[0]
    n = near[0].shape[0] // 2
    first = 0
    for here, there in zip(near, far):
        lanes = slice(first, first + here.shape[1])
        for k in range(4):
            ref = here if k < 2 else there
            rows = pl.ds(pl.multiple_of((row ^ k) * n, n), n)
            full[rows, lanes] = ref[(k % 2) * n : (k % 2 + 1) * n, :]
        first = lanes.stop
    lows[row] = low[...]
    for k, ref in ((1, r1), (2, r2), (3, r3)):
        lows[row ^ k] = load_terms(ref, offset, rank)
    total = (lows[0] + lows[1]) + (lows[2] + lows[3])
    whole = full[...]
    out[...] = adapter_scale * sum(
        jnp.dot(term, whole, preferred_element_type=f32) for term in split_terms(total)
    )


def small_kernel(
    own0, own1, mate0, mate1, low, hidden, up_act, down_act, o0, o1, o2, o3, *rest
):
    up_exit, down_entry, down_exit, full, ug = rest
    place_halves(ug, (own0, own1), (mate0, mate1))
    place_rows(full, (o0, o1, o2, o3), lax.axis_index("row"))
    up_exit[...] = adapter_scale * jnp.dot(up_act[...], ug[...], preferred_element_type=f32)
    down_entry[...] = adapter_scale * jnp.dot(
        low[...].astype(bf16), hidden[...], preferred_element_type=f32
    )
    down_exit[...] = adapter_scale * jnp.dot(down_act[...], full[...], preferred_element_type=f32)


def swap(x, axis, distance, n):
    return lax.ppermute(x, axis, [(i, i ^ distance) for i in range(n)])


EIGHTHS = (4,4)
CHUNKS = len(EIGHTHS)


def exchange_body(
    inputs,
    output_gradient,
    gate_preactivation,
    up_preactivation,
    gate_weight,
    up_weight,
    down_weight,
    up_adapter_entry,
    up_adapter_exit,
    down_adapter_entry,
    down_adapter_exit,
    up_adapter_activations,
    down_adapter_activations,
):
    tokens, hidden = gate_preactivation.shape
    share, width = output_gradient.shape
    rank = up_adapter_exit.shape[0]
    half = hidden // 2
    own_gradient = output_gradient
    gathered = [swap(own_gradient, "row", k, 4) for k in (1, 2, 3)]
    parts = [width // 8 * e for e in EIGHTHS]
    firsts = [sum(parts[:c]) for c in range(CHUNKS)]
    down_v = fetch(down_weight, 0, hidden)
    gate_v = [fetch(gate_weight, firsts[c], parts[c]) for c in range(CHUNKS)]
    up_v = [fetch(up_weight, firsts[c], parts[c]) for c in range(CHUNKS)]
    a, b, hidden_state = call(
        factors_kernel,
        (shape((tokens, hidden), f32), shape((tokens, hidden), f32), shape((tokens, hidden), bf16)),
        gate_preactivation,
        up_preactivation,
    )
    near = [call(stack_kernel, shape((2 * share, width), bf16), inputs, swap(inputs, "row", 1, 4))]
    down_v = after(down_v, gate_v, up_v, a, b, near)

    def hidden_half(flip, gradient, split):
        return call(
            functools.partial(hidden_kernel, flip, half, 256),
            (shape((tokens // split, half + LANES), f32),) * split,
            gradient,
            *gathered,
            in_vmem(down_v),
            down_adapter_exit,
            down_adapter_entry,
            scratch=[pltpu.VMEM((tokens, width), bf16)],
        )

    send = hidden_half(1, own_gradient, 4)
    got = [swap(x, "col", 1, 4) for x in send]
    keep = hidden_half(0, after(own_gradient, send), 1)[0]
    blocks = half // LANES
    far = [swap(near[0], "row", 2, 4)]
    payload = call(
        functools.partial(payload_kernel, rank, half),
        (
            shape((blocks // 2 * tokens + 3 * rank, LANES), bf16),
            shape((blocks // 2 * tokens, LANES), bf16),
        ),
        keep,
        *got,
    )
    other = [swap(x, "col", 2, 4) for x in payload]
    *grads, low_full = call(
        gradient_kernel,
        (shape((tokens // 2, half), bf16),) * 4 + (shape((rank, tokens), f32),),
        *payload,
        *other,
        a,
        b,
    )
    mate_grads = [swap(x, "col", 1, 4) for x in grads]

    owns, received = [], []
    outs = ()
    for c in range(CHUNKS):
        with_low = c == 0
        rows = parts[c] // LANES * share
        sent = shape((rows + (3 * rank if with_low else 0), LANES), bf16)
        outs = call(
            functools.partial(inputs_kernel, firsts[c], with_low, 512),
            (shape((share, parts[c]), f32), sent, sent, sent)
            + ((shape((rank, tokens), f32),) if with_low else ()),
            *grads,
            *mate_grads,
            in_vmem(after(gate_v[c], outs, far) if c else gate_v[c]),
            in_vmem(up_v[c]),
            up_adapter_exit,
            up_adapter_entry,
            scratch=[
                pltpu.VMEM((tokens, hidden), bf16),
                pltpu.VMEM((tokens, hidden), bf16),
                pltpu.VMEM((tokens, parts[c]), f32),
            ],
        )
        if with_low:
            low_up = outs[4]
        owns.append(outs[0])
        received.append([swap(outs[k], "row", k, 4) for k in (1, 2, 3)])
    input_grad = ()
    for c in range(CHUNKS):
        done = shape((share, firsts[c] + parts[c]), bf16)
        own = after(owns[c], owns[c + 1]) if c + 1 < CHUNKS else owns[c]
        input_grad = (call(finish_kernel, done, own, *received[c], *input_grad),)
    entry_sum = call(
        functools.partial(entry_kernel, parts[0] // LANES * share, 1),
        shape((rank, width), f32),
        after(low_up, owns),
        *received[0],
        *near,
        *far,
        scratch=[pltpu.VMEM((tokens, width), bf16), pltpu.VMEM((4, rank, tokens), f32)],
    )
    up_exit_gradient, down_entry_gradient, down_exit_gradient = call(
        small_kernel,
        (shape((rank, hidden), f32), shape((rank, hidden), f32), shape((rank, width), f32)),
        *grads[2:],
        *mate_grads[2:],
        low_full,
        hidden_state,
        up_adapter_activations,
        down_adapter_activations,
        own_gradient,
        *gathered,
        scratch=[pltpu.VMEM((tokens, width), bf16), pltpu.VMEM((tokens, hidden), bf16)],
    )
    return (
        input_grad[0],
        entry_sum,
        up_exit_gradient,
        down_entry_gradient,
        down_exit_gradient,
    )


def body(
    inputs,
    output_gradient,
    gate_preactivation,
    up_preactivation,
    gate_weight,
    up_weight,
    down_weight,
    up_adapter_entry,
    up_adapter_exit,
    down_adapter_entry,
    down_adapter_exit,
    up_adapter_activations,
    down_adapter_activations,
):
    highest_setting = HIGHEST
    complete_gradient = lax.all_gather(output_gradient, "row", axis=0, tiled=True)
    down_piece = contract_trailing(complete_gradient, down_adapter_exit)
    hidden_piece = contract_trailing(complete_gradient, down_weight)
    hidden_piece = hidden_piece + adapter_scale * jnp.dot(
        down_piece, down_adapter_entry.astype(f32), precision=highest_setting
    )
    hidden_gradient, down_full = lax.psum((hidden_piece, down_piece), "col")
    gate_f = gate_preactivation.astype(f32)
    up_f = up_preactivation.astype(f32)
    sigmoid_gate = jax.nn.sigmoid(gate_f)
    hidden_state = (gate_f * sigmoid_gate * up_f).astype(bf16)
    gate_grad = (
        hidden_gradient * up_f * sigmoid_gate * (1.0 + gate_f * (1.0 - sigmoid_gate))
    ).astype(bf16)
    up_gradient = (hidden_gradient * gate_f * sigmoid_gate).astype(bf16)
    down_rounded_value = down_full.astype(bf16)
    upper_piece = contract_trailing(up_gradient, up_adapter_exit)
    input_piece = contract_trailing(gate_grad, gate_weight) + contract_trailing(
        up_gradient, up_weight
    )
    input_piece = input_piece + adapter_scale * jnp.dot(
        upper_piece, up_adapter_entry.astype(f32), precision=highest_setting
    )
    input_grad, upper_full = (
        lax.psum_scatter(input_piece, "row", scatter_dimension=0, tiled=True),
        lax.psum_scatter(upper_piece, "row", scatter_dimension=0, tiled=True),
    )
    up_entry_term = adapter_scale * contract_leading(
        upper_full, inputs.astype(f32), matmul_accuracy=highest_setting
    )
    up_entry_gradient = lax.psum(up_entry_term, "row")
    up_exit_gradient = adapter_scale * jnp.dot(
        up_adapter_activations, up_gradient, preferred_element_type=f32
    )
    down_entry_gradient = adapter_scale * contract_leading(down_rounded_value, hidden_state)
    down_exit_gradient = adapter_scale * jnp.dot(
        down_adapter_activations, complete_gradient, preferred_element_type=f32
    )
    return (
        input_grad.astype(bf16),
        up_entry_gradient,
        up_exit_gradient,
        down_entry_gradient,
        down_exit_gradient,
    )


def solution(mesh):
    placed = (
        P(("grp", "row"), "col"),
        P(("grp", "row"), "col"),
        P("grp", "row"),
        P("grp", "row"),
        P("col", "row"),
        P("col", "row"),
        P("row", "col"),
        P(None, "col"),
        P(None, "row"),
        P(None, "row"),
        P(None, "col"),
        P(None, "grp"),
        P(None, "grp"),
    )
    exchange = mesh.shape["row"] == 4 and mesh.shape["col"] == 4
    return jax.shard_map(
        exchange_body if exchange else body,
        mesh=mesh,
        in_specs=placed,
        out_specs=(
            P(("grp", "row"), "col"),
            P("grp", "col"),
            P("grp", "row"),
            P("grp", "row"),
            P("grp", "col"),
        ),
        check_vma=False,
    )
```

```python
import functools

import jax
import jax.numpy as jnp
from jax import lax
from jax.experimental import pallas as pl
from jax.experimental.pallas import tpu as pltpu
from jax.sharding import PartitionSpec as P

adapter_scale = 2.0
HIGHEST = lax.Precision.HIGHEST
LANES = 128
VMEM_SPEC = pl.BlockSpec(memory_space=pltpu.VMEM)
HBM_SPEC = pl.BlockSpec(memory_space=pltpu.HBM)
f32 = jnp.float32
bf16 = jnp.bfloat16


def contract_trailing(left, right):
    return lax.dot_general(
        left, right, (((1,), (1,)), ((), ())), preferred_element_type=f32
    )


def contract_leading(left, right, matmul_accuracy=None):
    return lax.dot_general(
        left,
        right,
        (((0,), (0,)), ((), ())),
        precision=matmul_accuracy,
        preferred_element_type=f32,
    )


def in_vmem(x):
    return pltpu.with_memory_space_constraint(x, pltpu.VMEM)


def after(x, *others):
    return lax.optimization_barrier((x, *others))[0]


def call(kernel, out_shape, *args, scratch=(), specs=None, vmem=5 << 20):
    outs = out_shape if isinstance(out_shape, (tuple, list)) else (out_shape,)
    out_specs = tuple(VMEM_SPEC for _ in outs)
    result = pl.pallas_call(
        kernel,
        out_shape=tuple(outs),
        in_specs=specs if specs is not None else [VMEM_SPEC] * len(args),
        out_specs=out_specs,
        scratch_shapes=list(scratch),
        compiler_params=pltpu.CompilerParams(vmem_limit_bytes=vmem),
        cost_estimate=pl.CostEstimate(flops=0, transcendentals=0, bytes_accessed=0),
    )(*args)
    return result if isinstance(out_shape, (tuple, list)) else result[0]


def shape(dims, dtype):
    return jax.ShapeDtypeStruct(dims, dtype)


def fetch_kernel(pieces, first, src, dst, sems):
    rows = dst.shape[0] // pieces
    copies = [
        pltpu.make_async_copy(
            src.at[pl.ds(first + i * rows, rows)],
            dst.at[pl.ds(i * rows, rows)],
            sems.at[i],
        )
        for i in range(pieces)
    ]
    for c in copies:
        c.start()
    for c in copies:
        c.wait()


def fetch(weight, first, rows, pieces=4):
    return call(
        functools.partial(fetch_kernel, pieces, first),
        pltpu.VMEM((rows, weight.shape[1]), weight.dtype),
        pltpu.with_memory_space_constraint(weight, pltpu.HBM),
        scratch=[pltpu.SemaphoreType.DMA((pieces,))],
        specs=[HBM_SPEC],
        vmem=1 << 20,
    )


def factors_kernel(g_ref, u_ref, a_ref, b_ref, h_ref):
    g = g_ref[...].astype(f32)
    u = u_ref[...].astype(f32)
    q = 1.0 / (1.0 + jnp.exp(-g))
    b = g * q
    a_ref[...] = u * q * (1.0 + g * (1.0 - q))
    b_ref[...] = b
    h_ref[...] = (b * u).astype(bf16)


def split_terms(x):
    hi = x.astype(bf16)
    rest = x - hi.astype(f32)
    mid = rest.astype(bf16)
    low = (rest - mid.astype(f32)).astype(bf16)
    return hi, mid, low


def join_terms(hi, mid, low):
    return hi.astype(f32) + (mid.astype(f32) + low.astype(f32))


def store_terms(ref, start, x):
    n = x.shape[0]
    for i, term in enumerate(split_terms(x)):
        ref[start + i * n : start + (i + 1) * n, :] = term


def load_terms(ref, start, n):
    return join_terms(*(ref[start + i * n : start + (i + 1) * n, :] for i in range(3)))


def place_rows(full, pieces, position):
    n = pieces[0].shape[0]
    for k, piece in enumerate(pieces):
        full[pl.ds(pl.multiple_of((position ^ k) * n, n), n), :] = piece[...]


def hidden_block(full, low, w, entry, first, size):
    rows = pl.ds(pl.multiple_of(first, LANES), size)
    return contract_trailing(full[...], w[rows, :]) + adapter_scale * contract_leading(
        low, entry[:, rows].astype(f32), HIGHEST
    )


def send_kernel(half, block, o0, o1, o2, o3, w, exit_ref, entry, *outs):
    outs, low_ref, full = outs[:-2], outs[-2], outs[-1]
    n = outs[0].shape[0]
    place_rows(full, (o0, o1, o2, o3), lax.axis_index("row"))
    start = (1 - lax.rem(lax.axis_index("col"), 2)) * half
    low = contract_trailing(exit_ref[...], full[...])
    low_ref[...] = low
    outs[0][: low.shape[0], half:] = low
    for i in range(half // block):
        piece = hidden_block(full, low, w, entry, start + i * block, block)
        for j, out in enumerate(outs):
            out[:, i * block : (i + 1) * block] = piece[j * n : (j + 1) * n, :]


def keep_kernel(half, block, full, low, w, entry, out):
    start = lax.rem(lax.axis_index("col"), 2) * half
    for i in range(0, out.shape[1], block):
        size = min(block, out.shape[1] - i)
        out[:, i : i + size] = hidden_block(full, low[...], w, entry, start + i, size)


def store_blocks(out, piece, got, first):
    rows = piece.shape[0]
    for i in range(0, piece.shape[1], LANES):
        here = i // LANES * rows
        other = jnp.concatenate([ref[:, first + i : first + i + LANES] for ref in got], axis=0)
        out[here : here + rows, :] = (piece[:, i : i + LANES] + other).astype(bf16)


def payload_kernel(half, keep, low, *rest):
    got, out = rest[:-1], rest[-1]
    rank = low.shape[0]
    store_blocks(out, keep[...], got, 0)
    store_terms(out, out.shape[0] - 3 * rank, low[...] + got[0][:rank, half:])


def rest_kernel(half, first, full, low, w, entry, *rest):
    got, out = rest[:-1], rest[-1]
    start = lax.rem(lax.axis_index("col"), 2) * half + first
    piece = hidden_block(full, low[...], w, entry, start, half - first)
    store_blocks(out, piece, got, first)


def gradient_kernel(mine0, mine1, other0, other1, a, b, *outs):
    gate_outs, up_outs, low_ref = outs[:2], outs[2:4], outs[4]
    rows = a.shape[0]
    n, half = up_outs[0].shape
    rank = low_ref.shape[0]
    blocks = half // LANES
    later = mine1.shape[0] // rows
    start = pl.multiple_of(lax.rem(lax.axis_index("col"), 2) * half, half)
    for i in range(blocks):
        early = i < blocks - later
        k = i if early else i - (blocks - later)
        here = slice(k * rows, (k + 1) * rows)
        mine, other = (mine0, other0) if early else (mine1, other1)
        grad = mine[here, :].astype(f32) + other[here, :].astype(f32)
        lanes = pl.ds(pl.multiple_of(start + i * LANES, LANES), LANES)
        for refs, factor in ((gate_outs, a), (up_outs, b)):
            value = (grad * factor[:, lanes]).astype(bf16)
            for j, ref in enumerate(refs):
                ref[:, i * LANES : (i + 1) * LANES] = value[j * n : (j + 1) * n, :]
    terms = (blocks - later) * rows
    low_ref[...] = load_terms(mine0, terms, rank) + load_terms(other0, terms, rank)


def place_halves(full, own, mate):
    n, half = own[0].shape
    par = lax.rem(lax.axis_index("col"), 2)
    for position, refs in ((par, own), (1 - par, mate)):
        lanes = pl.ds(pl.multiple_of(position * half, half), half)
        for j, ref in enumerate(refs):
            full[j * n : (j + 1) * n, lanes] = ref[...]


def inputs_kernel(first, with_low, block, *refs):
    own, mate, (wg, wu, exit_ref, entry), rest = refs[:4], refs[4:8], refs[8:12], refs[12:]
    own_out, s1, s2, s3 = rest[:4]
    low_ref = rest[4] if with_low else None
    gg, ug, acc = rest[-3:]
    width = acc.shape[1]
    rank = exit_ref.shape[0]
    place_halves(gg, own[:2], mate[:2])
    place_halves(ug, own[2:], mate[2:])
    low = contract_trailing(exit_ref[...], ug[...])
    for i in range(width // block):
        rows = slice(i * block, (i + 1) * block)
        lanes = slice(first + i * block, first + (i + 1) * block)
        acc[:, i * block : (i + 1) * block] = (
            contract_trailing(gg[...], wg[rows, :])
            + contract_trailing(ug[...], wu[rows, :])
            + adapter_scale * contract_leading(low, entry[:, lanes].astype(f32), HIGHEST)
        )
    row = lax.axis_index("row")
    n = own_out.shape[0]
    own_out[...] = acc[pl.ds(pl.multiple_of(row * n, n), n), :]
    for k, out in ((1, s1), (2, s2), (3, s3)):
        dest = pl.ds(pl.multiple_of((row ^ k) * n, n), n)
        for i in range(width // LANES):
            out[i * n : (i + 1) * n, :] = acc[dest, i * LANES : (i + 1) * LANES].astype(bf16)
        if with_low:
            store_terms(out, width // LANES * n, low)
    if with_low:
        low_ref[...] = low


def finish_kernel(own, r1, r2, r3, *rest):
    done, out = rest[:-1], rest[-1]
    n, width = own.shape
    first = out.shape[1] - width
    for ref in done:
        out[:, :first] = ref[...]
    for i in range(width // LANES):
        here = slice(i * n, (i + 1) * n)
        lanes = slice(i * LANES, (i + 1) * LANES)
        out[:, first + i * LANES : first + (i + 1) * LANES] = (
            own[:, lanes]
            + r1[here, :].astype(f32)
            + r2[here, :].astype(f32)
            + r3[here, :].astype(f32)
        ).astype(bf16)


def stack_kernel(top, bottom, *outs):
    n = top.shape[0]
    first = 0
    for out in outs:
        lanes = slice(first, first + out.shape[1])
        out[:n, :] = top[:, lanes]
        out[n:, :] = bottom[:, lanes]
        first = lanes.stop


def entry_kernel(offset, pieces, low, r1, r2, r3, *rest):
    near, far = rest[:pieces], rest[pieces : 2 * pieces]
    out, full, lows = rest[2 * pieces :]
    row = lax.axis_index("row")
    rank = low.shape[0]
    n = near[0].shape[0] // 2
    first = 0
    for here, there in zip(near, far):
        lanes = slice(first, first + here.shape[1])
        for k in range(4):
            ref = here if k < 2 else there
            rows = pl.ds(pl.multiple_of((row ^ k) * n, n), n)
            full[rows, lanes] = ref[(k % 2) * n : (k % 2 + 1) * n, :]
        first = lanes.stop
    lows[row] = low[...]
    for k, ref in ((1, r1), (2, r2), (3, r3)):
        lows[row ^ k] = load_terms(ref, offset, rank)
    total = (lows[0] + lows[1]) + (lows[2] + lows[3])
    whole = full[...]
    out[...] = adapter_scale * sum(
        jnp.dot(term, whole, preferred_element_type=f32) for term in split_terms(total)
    )


def small_kernel(own0, own1, mate0, mate1, low, hidden, up_act, down_act, full, *rest):
    up_exit, down_entry, down_exit, ug = rest
    place_halves(ug, (own0, own1), (mate0, mate1))
    up_exit[...] = adapter_scale * jnp.dot(up_act[...], ug[...], preferred_element_type=f32)
    down_entry[...] = adapter_scale * jnp.dot(
        low[...].astype(bf16), hidden[...], preferred_element_type=f32
    )
    down_exit[...] = adapter_scale * jnp.dot(down_act[...], full[...], preferred_element_type=f32)


def swap(x, axis, distance, n):
    return lax.ppermute(x, axis, [(i, i ^ distance) for i in range(n)])


EIGHTHS = (4,4)
CHUNKS = len(EIGHTHS)
KEEP_EIGHTHS = 5


def exchange_body(
    inputs,
    output_gradient,
    gate_preactivation,
    up_preactivation,
    gate_weight,
    up_weight,
    down_weight,
    up_adapter_entry,
    up_adapter_exit,
    down_adapter_entry,
    down_adapter_exit,
    up_adapter_activations,
    down_adapter_activations,
):
    tokens, hidden = gate_preactivation.shape
    share, width = output_gradient.shape
    rank = up_adapter_exit.shape[0]
    half = hidden // 2
    own_gradient = output_gradient
    gathered = [swap(own_gradient, "row", k, 4) for k in (1, 2, 3)]
    parts = [width // 8 * e for e in EIGHTHS]
    firsts = [sum(parts[:c]) for c in range(CHUNKS)]
    down_v = fetch(down_weight, 0, hidden)
    gate_v = [fetch(gate_weight, firsts[c], parts[c]) for c in range(CHUNKS)]
    up_v = [fetch(up_weight, firsts[c], parts[c]) for c in range(CHUNKS)]
    a, b, hidden_state = call(
        factors_kernel,
        (shape((tokens, hidden), f32), shape((tokens, hidden), f32), shape((tokens, hidden), bf16)),
        gate_preactivation,
        up_preactivation,
    )
    near = [call(stack_kernel, shape((2 * share, width), bf16), inputs, swap(inputs, "row", 1, 4))]
    down_v = after(down_v, gate_v, up_v, a, b, near)

    quarter = shape((tokens // 4, half + LANES), f32)
    *send, low_piece, full_gradient = call(
        functools.partial(send_kernel, half, 256),
        (quarter,) * 4 + (shape((rank, tokens), f32), shape((tokens, width), bf16)),
        own_gradient,
        *gathered,
        in_vmem(down_v),
        down_adapter_exit,
        down_adapter_entry,
    )
    got = [swap(x, "col", 1, 4) for x in send]
    far = [swap(near[0], "row", 2, 4)]
    first = half // 8 * KEEP_EIGHTHS
    keep = call(
        functools.partial(keep_kernel, half, 256),
        shape((tokens, first), f32),
        full_gradient,
        low_piece,
        in_vmem(down_v),
        down_adapter_entry,
    )
    early = call(
        functools.partial(payload_kernel, half),
        shape((first // LANES * tokens + 3 * rank, LANES), bf16),
        keep,
        low_piece,
        *got,
    )
    late = call(
        functools.partial(rest_kernel, half, first),
        shape(((half - first) // LANES * tokens, LANES), bf16),
        after(full_gradient, early),
        low_piece,
        in_vmem(down_v),
        down_adapter_entry,
        *got,
    )
    payload = (early, late)
    other = [swap(x, "col", 2, 4) for x in payload]
    *grads, low_full = call(
        gradient_kernel,
        (shape((tokens // 2, half), bf16),) * 4 + (shape((rank, tokens), f32),),
        *payload,
        *other,
        a,
        b,
    )
    mate_grads = [swap(x, "col", 1, 4) for x in grads]

    owns, received = [], []
    outs = ()
    for c in range(CHUNKS):
        with_low = c == 0
        rows = parts[c] // LANES * share
        sent = shape((rows + (3 * rank if with_low else 0), LANES), bf16)
        outs = call(
            functools.partial(inputs_kernel, firsts[c], with_low, 512),
            (shape((share, parts[c]), f32), sent, sent, sent)
            + ((shape((rank, tokens), f32),) if with_low else ()),
            *grads,
            *mate_grads,
            in_vmem(after(gate_v[c], outs, far) if c else gate_v[c]),
            in_vmem(up_v[c]),
            up_adapter_exit,
            up_adapter_entry,
            scratch=[
                pltpu.VMEM((tokens, hidden), bf16),
                pltpu.VMEM((tokens, hidden), bf16),
                pltpu.VMEM((tokens, parts[c]), f32),
            ],
        )
        if with_low:
            low_up = outs[4]
        owns.append(outs[0])
        received.append([swap(outs[k], "row", k, 4) for k in (1, 2, 3)])
    input_grad = ()
    for c in range(CHUNKS):
        done = shape((share, firsts[c] + parts[c]), bf16)
        own = after(owns[c], owns[c + 1]) if c + 1 < CHUNKS else owns[c]
        input_grad = (call(finish_kernel, done, own, *received[c], *input_grad),)
    entry_sum = call(
        functools.partial(entry_kernel, parts[0] // LANES * share, 1),
        shape((rank, width), f32),
        after(low_up, owns),
        *received[0],
        *near,
        *far,
        scratch=[pltpu.VMEM((tokens, width), bf16), pltpu.VMEM((4, rank, tokens), f32)],
    )
    up_exit_gradient, down_entry_gradient, down_exit_gradient = call(
        small_kernel,
        (shape((rank, hidden), f32), shape((rank, hidden), f32), shape((rank, width), f32)),
        *grads[2:],
        *mate_grads[2:],
        low_full,
        hidden_state,
        up_adapter_activations,
        down_adapter_activations,
        full_gradient,
        scratch=[pltpu.VMEM((tokens, hidden), bf16)],
    )
    return (
        input_grad[0],
        entry_sum,
        up_exit_gradient,
        down_entry_gradient,
        down_exit_gradient,
    )


def body(
    inputs,
    output_gradient,
    gate_preactivation,
    up_preactivation,
    gate_weight,
    up_weight,
    down_weight,
    up_adapter_entry,
    up_adapter_exit,
    down_adapter_entry,
    down_adapter_exit,
    up_adapter_activations,
    down_adapter_activations,
):
    highest_setting = HIGHEST
    complete_gradient = lax.all_gather(output_gradient, "row", axis=0, tiled=True)
    down_piece = contract_trailing(complete_gradient, down_adapter_exit)
    hidden_piece = contract_trailing(complete_gradient, down_weight)
    hidden_piece = hidden_piece + adapter_scale * jnp.dot(
        down_piece, down_adapter_entry.astype(f32), precision=highest_setting
    )
    hidden_gradient, down_full = lax.psum((hidden_piece, down_piece), "col")
    gate_f = gate_preactivation.astype(f32)
    up_f = up_preactivation.astype(f32)
    sigmoid_gate = jax.nn.sigmoid(gate_f)
    hidden_state = (gate_f * sigmoid_gate * up_f).astype(bf16)
    gate_grad = (
        hidden_gradient * up_f * sigmoid_gate * (1.0 + gate_f * (1.0 - sigmoid_gate))
    ).astype(bf16)
    up_gradient = (hidden_gradient * gate_f * sigmoid_gate).astype(bf16)
    down_rounded_value = down_full.astype(bf16)
    upper_piece = contract_trailing(up_gradient, up_adapter_exit)
    input_piece = contract_trailing(gate_grad, gate_weight) + contract_trailing(
        up_gradient, up_weight
    )
    input_piece = input_piece + adapter_scale * jnp.dot(
        upper_piece, up_adapter_entry.astype(f32), precision=highest_setting
    )
    input_grad, upper_full = (
        lax.psum_scatter(input_piece, "row", scatter_dimension=0, tiled=True),
        lax.psum_scatter(upper_piece, "row", scatter_dimension=0, tiled=True),
    )
    up_entry_term = adapter_scale * contract_leading(
        upper_full, inputs.astype(f32), matmul_accuracy=highest_setting
    )
    up_entry_gradient = lax.psum(up_entry_term, "row")
    up_exit_gradient = adapter_scale * jnp.dot(
        up_adapter_activations, up_gradient, preferred_element_type=f32
    )
    down_entry_gradient = adapter_scale * contract_leading(down_rounded_value, hidden_state)
    down_exit_gradient = adapter_scale * jnp.dot(
        down_adapter_activations, complete_gradient, preferred_element_type=f32
    )
    return (
        input_grad.astype(bf16),
        up_entry_gradient,
        up_exit_gradient,
        down_entry_gradient,
        down_exit_gradient,
    )


def solution(mesh):
    placed = (
        P(("grp", "row"), "col"),
        P(("grp", "row"), "col"),
        P("grp", "row"),
        P("grp", "row"),
        P("col", "row"),
        P("col", "row"),
        P("row", "col"),
        P(None, "col"),
        P(None, "row"),
        P(None, "row"),
        P(None, "col"),
        P(None, "grp"),
        P(None, "grp"),
    )
    exchange = mesh.shape["row"] == 4 and mesh.shape["col"] == 4
    return jax.shard_map(
        exchange_body if exchange else body,
        mesh=mesh,
        in_specs=placed,
        out_specs=(
            P(("grp", "row"), "col"),
            P("grp", "col"),
            P("grp", "row"),
            P("grp", "row"),
            P("grp", "col"),
        ),
        check_vma=False,
    )
```

```python
import functools

import jax
import jax.numpy as jnp
from jax import lax
from jax.experimental import pallas as pl
from jax.experimental.pallas import tpu as pltpu
from jax.sharding import PartitionSpec as P

adapter_scale = 2.0
HIGHEST = lax.Precision.HIGHEST
LANES = 128
VMEM_SPEC = pl.BlockSpec(memory_space=pltpu.VMEM)
HBM_SPEC = pl.BlockSpec(memory_space=pltpu.HBM)
f32 = jnp.float32
bf16 = jnp.bfloat16


def contract_trailing(left, right):
    return lax.dot_general(
        left, right, (((1,), (1,)), ((), ())), preferred_element_type=f32
    )


def contract_leading(left, right, matmul_accuracy=None):
    return lax.dot_general(
        left,
        right,
        (((0,), (0,)), ((), ())),
        precision=matmul_accuracy,
        preferred_element_type=f32,
    )


def in_vmem(x):
    return pltpu.with_memory_space_constraint(x, pltpu.VMEM)


def after(x, *others):
    return lax.optimization_barrier((x, *others))[0]


def call(kernel, out_shape, *args, scratch=(), specs=None, vmem=5 << 20):
    outs = out_shape if isinstance(out_shape, (tuple, list)) else (out_shape,)
    out_specs = tuple(VMEM_SPEC for _ in outs)
    result = pl.pallas_call(
        kernel,
        out_shape=tuple(outs),
        in_specs=specs if specs is not None else [VMEM_SPEC] * len(args),
        out_specs=out_specs,
        scratch_shapes=list(scratch),
        compiler_params=pltpu.CompilerParams(vmem_limit_bytes=vmem),
        cost_estimate=pl.CostEstimate(flops=0, transcendentals=0, bytes_accessed=0),
    )(*args)
    return result if isinstance(out_shape, (tuple, list)) else result[0]


def shape(dims, dtype):
    return jax.ShapeDtypeStruct(dims, dtype)


def fetch_kernel(pieces, first, src, dst, sems):
    rows = dst.shape[0] // pieces
    copies = [
        pltpu.make_async_copy(
            src.at[pl.ds(first + i * rows, rows)],
            dst.at[pl.ds(i * rows, rows)],
            sems.at[i],
        )
        for i in range(pieces)
    ]
    for c in copies:
        c.start()
    for c in copies:
        c.wait()


def fetch(weight, first, rows, pieces=4):
    return call(
        functools.partial(fetch_kernel, pieces, first),
        pltpu.VMEM((rows, weight.shape[1]), weight.dtype),
        pltpu.with_memory_space_constraint(weight, pltpu.HBM),
        scratch=[pltpu.SemaphoreType.DMA((pieces,))],
        specs=[HBM_SPEC],
        vmem=1 << 20,
    )


def factors_kernel(g_ref, u_ref, a_ref, b_ref, h_ref):
    g = g_ref[...].astype(f32)
    u = u_ref[...].astype(f32)
    q = 1.0 / (1.0 + jnp.exp(-g))
    b = g * q
    a_ref[...] = u * q * (1.0 + g * (1.0 - q))
    b_ref[...] = b
    h_ref[...] = (b * u).astype(bf16)


def split_terms(x):
    hi = x.astype(bf16)
    rest = x - hi.astype(f32)
    mid = rest.astype(bf16)
    low = (rest - mid.astype(f32)).astype(bf16)
    return hi, mid, low


def join_terms(hi, mid, low):
    return hi.astype(f32) + (mid.astype(f32) + low.astype(f32))


def store_terms(ref, start, x):
    n = x.shape[0]
    for i, term in enumerate(split_terms(x)):
        ref[start + i * n : start + (i + 1) * n, :] = term


def load_terms(ref, start, n):
    return join_terms(*(ref[start + i * n : start + (i + 1) * n, :] for i in range(3)))


def place_rows(full, pieces, position):
    n = pieces[0].shape[0]
    for k, piece in enumerate(pieces):
        full[pl.ds(pl.multiple_of((position ^ k) * n, n), n), :] = piece[...]


def hidden_block(full, low, w, entry, first, size):
    rows = pl.ds(pl.multiple_of(first, LANES), size)
    return contract_trailing(full[...], w[rows, :]) + adapter_scale * contract_leading(
        low, entry[:, rows].astype(f32), HIGHEST
    )


def send_kernel(half, block, o0, o1, o2, o3, w, exit_ref, entry, *outs):
    outs, low_ref, full = outs[:-2], outs[-2], outs[-1]
    n = outs[0].shape[0]
    place_rows(full, (o0, o1, o2, o3), lax.axis_index("row"))
    start = (1 - lax.rem(lax.axis_index("col"), 2)) * half
    low = contract_trailing(exit_ref[...], full[...])
    low_ref[...] = low
    outs[0][: low.shape[0], half:] = low
    for i in range(half // block):
        piece = hidden_block(full, low, w, entry, start + i * block, block)
        for j, out in enumerate(outs):
            out[:, i * block : (i + 1) * block] = piece[j * n : (j + 1) * n, :]


def keep_kernel(half, block, full, low, w, entry, out):
    start = lax.rem(lax.axis_index("col"), 2) * half
    for i in range(0, out.shape[1], block):
        size = min(block, out.shape[1] - i)
        out[:, i : i + size] = hidden_block(full, low[...], w, entry, start + i, size)


def store_blocks(out, piece, got, first):
    rows = piece.shape[0]
    for i in range(0, piece.shape[1], LANES):
        here = i // LANES * rows
        other = jnp.concatenate([ref[:, first + i : first + i + LANES] for ref in got], axis=0)
        out[here : here + rows, :] = (piece[:, i : i + LANES] + other).astype(bf16)


def payload_kernel(half, keep, low, *rest):
    got, out = rest[:-1], rest[-1]
    rank = low.shape[0]
    store_blocks(out, keep[...], got, 0)
    store_terms(out, out.shape[0] - 3 * rank, low[...] + got[0][:rank, half:])


def rest_kernel(half, first, full, low, w, entry, *rest):
    got, out = rest[:-1], rest[-1]
    start = lax.rem(lax.axis_index("col"), 2) * half + first
    piece = hidden_block(full, low[...], w, entry, start, half - first)
    store_blocks(out, piece, got, first)


def gradient_kernel(mine0, mine1, other0, other1, a, b, *outs):
    gate_outs, up_outs, low_ref = outs[:2], outs[2:4], outs[4]
    rows = a.shape[0]
    n, half = up_outs[0].shape
    rank = low_ref.shape[0]
    blocks = half // LANES
    later = mine1.shape[0] // rows
    start = pl.multiple_of(lax.rem(lax.axis_index("col"), 2) * half, half)
    for i in range(blocks):
        early = i < blocks - later
        k = i if early else i - (blocks - later)
        here = slice(k * rows, (k + 1) * rows)
        mine, other = (mine0, other0) if early else (mine1, other1)
        grad = mine[here, :].astype(f32) + other[here, :].astype(f32)
        lanes = pl.ds(pl.multiple_of(start + i * LANES, LANES), LANES)
        for refs, factor in ((gate_outs, a), (up_outs, b)):
            value = (grad * factor[:, lanes]).astype(bf16)
            for j, ref in enumerate(refs):
                ref[:, i * LANES : (i + 1) * LANES] = value[j * n : (j + 1) * n, :]
    terms = (blocks - later) * rows
    low_ref[...] = load_terms(mine0, terms, rank) + load_terms(other0, terms, rank)


def place_halves(full, own, mate):
    n, half = own[0].shape
    par = lax.rem(lax.axis_index("col"), 2)
    for position, refs in ((par, own), (1 - par, mate)):
        lanes = pl.ds(pl.multiple_of(position * half, half), half)
        for j, ref in enumerate(refs):
            full[j * n : (j + 1) * n, lanes] = ref[...]


def inputs_kernel(first, with_low, block, *refs):
    own, mate, (wg, wu, exit_ref, entry), rest = refs[:4], refs[4:8], refs[8:12], refs[12:]
    own_out, s1, s2, s3 = rest[:4]
    low_ref = rest[4] if with_low else None
    gg, ug, acc = rest[-3:]
    width = acc.shape[1]
    rank = exit_ref.shape[0]
    place_halves(gg, own[:2], mate[:2])
    place_halves(ug, own[2:], mate[2:])
    low = contract_trailing(exit_ref[...], ug[...])
    for i in range(width // block):
        rows = slice(i * block, (i + 1) * block)
        lanes = slice(first + i * block, first + (i + 1) * block)
        acc[:, i * block : (i + 1) * block] = (
            contract_trailing(gg[...], wg[rows, :])
            + contract_trailing(ug[...], wu[rows, :])
            + adapter_scale * contract_leading(low, entry[:, lanes].astype(f32), HIGHEST)
        )
    row = lax.axis_index("row")
    n = own_out.shape[0]
    own_out[...] = acc[pl.ds(pl.multiple_of(row * n, n), n), :]
    for k, out in ((1, s1), (2, s2), (3, s3)):
        dest = pl.ds(pl.multiple_of((row ^ k) * n, n), n)
        for i in range(width // LANES):
            out[i * n : (i + 1) * n, :] = acc[dest, i * LANES : (i + 1) * LANES].astype(bf16)
        if with_low:
            store_terms(out, width // LANES * n, low)
    if with_low:
        low_ref[...] = low


def finish_kernel(own, r1, r2, r3, *rest):
    done, out = rest[:-1], rest[-1]
    n, width = own.shape
    first = out.shape[1] - width
    for ref in done:
        out[:, :first] = ref[...]
    for i in range(width // LANES):
        here = slice(i * n, (i + 1) * n)
        lanes = slice(i * LANES, (i + 1) * LANES)
        out[:, first + i * LANES : first + (i + 1) * LANES] = (
            own[:, lanes]
            + r1[here, :].astype(f32)
            + r2[here, :].astype(f32)
            + r3[here, :].astype(f32)
        ).astype(bf16)


def entry_kernel(offset, low, r1, r2, r3, i0, i1, i2, i3, out, full, lows):
    row = lax.axis_index("row")
    rank = low.shape[0]
    place_rows(full, (i0, i1, i2, i3), row)
    lows[row] = low[...]
    for k, ref in ((1, r1), (2, r2), (3, r3)):
        lows[row ^ k] = load_terms(ref, offset, rank)
    total = (lows[0] + lows[1]) + (lows[2] + lows[3])
    whole = full[...]
    out[...] = adapter_scale * sum(
        jnp.dot(term, whole, preferred_element_type=f32) for term in split_terms(total)
    )


def small_kernel(own0, own1, mate0, mate1, low, hidden, up_act, down_act, full, *rest):
    up_exit, down_entry, down_exit, ug = rest
    place_halves(ug, (own0, own1), (mate0, mate1))
    up_exit[...] = adapter_scale * jnp.dot(up_act[...], ug[...], preferred_element_type=f32)
    down_entry[...] = adapter_scale * jnp.dot(
        low[...].astype(bf16), hidden[...], preferred_element_type=f32
    )
    down_exit[...] = adapter_scale * jnp.dot(down_act[...], full[...], preferred_element_type=f32)


def swap(x, axis, distance, n):
    return lax.ppermute(x, axis, [(i, i ^ distance) for i in range(n)])


EIGHTHS = (4,4)
CHUNKS = len(EIGHTHS)
KEEP_EIGHTHS = 5


def exchange_body(
    inputs,
    output_gradient,
    gate_preactivation,
    up_preactivation,
    gate_weight,
    up_weight,
    down_weight,
    up_adapter_entry,
    up_adapter_exit,
    down_adapter_entry,
    down_adapter_exit,
    up_adapter_activations,
    down_adapter_activations,
):
    tokens, hidden = gate_preactivation.shape
    share, width = output_gradient.shape
    rank = up_adapter_exit.shape[0]
    half = hidden // 2
    own_gradient = output_gradient
    gathered = [swap(own_gradient, "row", k, 4) for k in (1, 2)]
    parts = [width // 8 * e for e in EIGHTHS]
    firsts = [sum(parts[:c]) for c in range(CHUNKS)]
    down_v = fetch(down_weight, 0, hidden)
    gate_v = [fetch(gate_weight, firsts[c], parts[c]) for c in range(CHUNKS)]
    up_v = [fetch(up_weight, firsts[c], parts[c]) for c in range(CHUNKS - 1)]
    near = swap(inputs, "row", 1, 4)
    gathered.append(swap(after(gathered[1], gate_v, up_v, near), "row", 1, 4))
    down_v = after(down_v, gate_v, up_v, near)

    quarter = shape((tokens // 4, half + LANES), f32)
    *send, low_piece, full_gradient = call(
        functools.partial(send_kernel, half, 256),
        (quarter,) * 4 + (shape((rank, tokens), f32), shape((tokens, width), bf16)),
        own_gradient,
        *gathered,
        in_vmem(down_v),
        down_adapter_exit,
        down_adapter_entry,
    )
    got = [swap(x, "col", 1, 4) for x in send]
    far = swap(after(inputs, gathered, near), "row", 2, 4)
    last = swap(far, "row", 1, 4)
    first = half // 8 * KEEP_EIGHTHS
    keep = call(
        functools.partial(keep_kernel, half, 256),
        shape((tokens, first), f32),
        full_gradient,
        low_piece,
        in_vmem(down_v),
        down_adapter_entry,
    )
    early = call(
        functools.partial(payload_kernel, half),
        shape((first // LANES * tokens + 3 * rank, LANES), bf16),
        keep,
        low_piece,
        *got,
    )
    late = call(
        functools.partial(rest_kernel, half, first),
        shape(((half - first) // LANES * tokens, LANES), bf16),
        after(full_gradient, early),
        low_piece,
        in_vmem(down_v),
        down_adapter_entry,
        *got,
    )
    payload = (early, late)
    other = [swap(x, "col", 2, 4) for x in payload]
    up_v.append(fetch(after(up_weight, payload), firsts[-1], parts[-1]))
    a, b, hidden_state = call(
        factors_kernel,
        (shape((tokens, hidden), f32), shape((tokens, hidden), f32), shape((tokens, hidden), bf16)),
        after(gate_preactivation, payload),
        up_preactivation,
    )
    *grads, low_full = call(
        gradient_kernel,
        (shape((tokens // 2, half), bf16),) * 4 + (shape((rank, tokens), f32),),
        *payload,
        *other,
        after(a, up_v),
        b,
    )
    mate_grads = [swap(x, "col", 1, 4) for x in grads]

    owns, received = [], []
    outs = ()
    for c in range(CHUNKS):
        with_low = c == 0
        rows = parts[c] // LANES * share
        sent = shape((rows + (3 * rank if with_low else 0), LANES), bf16)
        outs = call(
            functools.partial(inputs_kernel, firsts[c], with_low, 512),
            (shape((share, parts[c]), f32), sent, sent, sent)
            + ((shape((rank, tokens), f32),) if with_low else ()),
            *grads,
            *mate_grads,
            in_vmem(after(gate_v[c], outs, last) if c else gate_v[c]),
            in_vmem(up_v[c]),
            up_adapter_exit,
            up_adapter_entry,
            scratch=[
                pltpu.VMEM((tokens, hidden), bf16),
                pltpu.VMEM((tokens, hidden), bf16),
                pltpu.VMEM((tokens, parts[c]), f32),
            ],
        )
        if with_low:
            low_up = outs[4]
        owns.append(outs[0])
        received.append([swap(outs[k], "row", k, 4) for k in (1, 2, 3)])
    input_grad = ()
    for c in range(CHUNKS):
        done = shape((share, firsts[c] + parts[c]), bf16)
        own = after(owns[c], owns[c + 1]) if c + 1 < CHUNKS else owns[c]
        input_grad = (call(finish_kernel, done, own, *received[c], *input_grad),)
    entry_sum = call(
        functools.partial(entry_kernel, parts[0] // LANES * share),
        shape((rank, width), f32),
        after(low_up, owns),
        *received[0],
        inputs,
        near,
        far,
        last,
        scratch=[pltpu.VMEM((tokens, width), bf16), pltpu.VMEM((4, rank, tokens), f32)],
    )
    up_exit_gradient, down_entry_gradient, down_exit_gradient = call(
        small_kernel,
        (shape((rank, hidden), f32), shape((rank, hidden), f32), shape((rank, width), f32)),
        *grads[2:],
        *mate_grads[2:],
        low_full,
        hidden_state,
        up_adapter_activations,
        down_adapter_activations,
        full_gradient,
        scratch=[pltpu.VMEM((tokens, hidden), bf16)],
    )
    return (
        input_grad[0],
        entry_sum,
        up_exit_gradient,
        down_entry_gradient,
        down_exit_gradient,
    )


def body(
    inputs,
    output_gradient,
    gate_preactivation,
    up_preactivation,
    gate_weight,
    up_weight,
    down_weight,
    up_adapter_entry,
    up_adapter_exit,
    down_adapter_entry,
    down_adapter_exit,
    up_adapter_activations,
    down_adapter_activations,
):
    highest_setting = HIGHEST
    complete_gradient = lax.all_gather(output_gradient, "row", axis=0, tiled=True)
    down_piece = contract_trailing(complete_gradient, down_adapter_exit)
    hidden_piece = contract_trailing(complete_gradient, down_weight)
    hidden_piece = hidden_piece + adapter_scale * jnp.dot(
        down_piece, down_adapter_entry.astype(f32), precision=highest_setting
    )
    hidden_gradient, down_full = lax.psum((hidden_piece, down_piece), "col")
    gate_f = gate_preactivation.astype(f32)
    up_f = up_preactivation.astype(f32)
    sigmoid_gate = jax.nn.sigmoid(gate_f)
    hidden_state = (gate_f * sigmoid_gate * up_f).astype(bf16)
    gate_grad = (
        hidden_gradient * up_f * sigmoid_gate * (1.0 + gate_f * (1.0 - sigmoid_gate))
    ).astype(bf16)
    up_gradient = (hidden_gradient * gate_f * sigmoid_gate).astype(bf16)
    down_rounded_value = down_full.astype(bf16)
    upper_piece = contract_trailing(up_gradient, up_adapter_exit)
    input_piece = contract_trailing(gate_grad, gate_weight) + contract_trailing(
        up_gradient, up_weight
    )
    input_piece = input_piece + adapter_scale * jnp.dot(
        upper_piece, up_adapter_entry.astype(f32), precision=highest_setting
    )
    input_grad, upper_full = (
        lax.psum_scatter(input_piece, "row", scatter_dimension=0, tiled=True),
        lax.psum_scatter(upper_piece, "row", scatter_dimension=0, tiled=True),
    )
    up_entry_term = adapter_scale * contract_leading(
        upper_full, inputs.astype(f32), matmul_accuracy=highest_setting
    )
    up_entry_gradient = lax.psum(up_entry_term, "row")
    up_exit_gradient = adapter_scale * jnp.dot(
        up_adapter_activations, up_gradient, preferred_element_type=f32
    )
    down_entry_gradient = adapter_scale * contract_leading(down_rounded_value, hidden_state)
    down_exit_gradient = adapter_scale * jnp.dot(
        down_adapter_activations, complete_gradient, preferred_element_type=f32
    )
    return (
        input_grad.astype(bf16),
        up_entry_gradient,
        up_exit_gradient,
        down_entry_gradient,
        down_exit_gradient,
    )


def solution(mesh):
    placed = (
        P(("grp", "row"), "col"),
        P(("grp", "row"), "col"),
        P("grp", "row"),
        P("grp", "row"),
        P("col", "row"),
        P("col", "row"),
        P("row", "col"),
        P(None, "col"),
        P(None, "row"),
        P(None, "row"),
        P(None, "col"),
        P(None, "grp"),
        P(None, "grp"),
    )
    exchange = mesh.shape["row"] == 4 and mesh.shape["col"] == 4
    return jax.shard_map(
        exchange_body if exchange else body,
        mesh=mesh,
        in_specs=placed,
        out_specs=(
            P(("grp", "row"), "col"),
            P("grp", "col"),
            P("grp", "row"),
            P("grp", "row"),
            P("grp", "col"),
        ),
        check_vma=False,
    )
```

```python
import functools

import jax
import jax.numpy as jnp
from jax import lax
from jax.experimental import pallas as pl
from jax.experimental.pallas import tpu as pltpu
from jax.sharding import PartitionSpec as P

adapter_scale = 2.0
HIGHEST = lax.Precision.HIGHEST
LANES = 128
VMEM_SPEC = pl.BlockSpec(memory_space=pltpu.VMEM)
HBM_SPEC = pl.BlockSpec(memory_space=pltpu.HBM)
f32 = jnp.float32
bf16 = jnp.bfloat16


def contract_trailing(left, right):
    return lax.dot_general(
        left, right, (((1,), (1,)), ((), ())), preferred_element_type=f32
    )


def contract_leading(left, right, matmul_accuracy=None):
    return lax.dot_general(
        left,
        right,
        (((0,), (0,)), ((), ())),
        precision=matmul_accuracy,
        preferred_element_type=f32,
    )


def in_vmem(x):
    return pltpu.with_memory_space_constraint(x, pltpu.VMEM)


def after(x, *others):
    return lax.optimization_barrier((x, *others))[0]


def call(kernel, out_shape, *args, scratch=(), specs=None, vmem=5 << 20):
    outs = out_shape if isinstance(out_shape, (tuple, list)) else (out_shape,)
    out_specs = tuple(VMEM_SPEC for _ in outs)
    result = pl.pallas_call(
        kernel,
        out_shape=tuple(outs),
        in_specs=specs if specs is not None else [VMEM_SPEC] * len(args),
        out_specs=out_specs,
        scratch_shapes=list(scratch),
        compiler_params=pltpu.CompilerParams(vmem_limit_bytes=vmem),
        cost_estimate=pl.CostEstimate(flops=0, transcendentals=0, bytes_accessed=0),
    )(*args)
    return result if isinstance(out_shape, (tuple, list)) else result[0]


def shape(dims, dtype):
    return jax.ShapeDtypeStruct(dims, dtype)


def fetch_kernel(pieces, first, src, dst, sems):
    rows = dst.shape[0] // pieces
    copies = [
        pltpu.make_async_copy(
            src.at[pl.ds(first + i * rows, rows)],
            dst.at[pl.ds(i * rows, rows)],
            sems.at[i],
        )
        for i in range(pieces)
    ]
    for c in copies:
        c.start()
    for c in copies:
        c.wait()


def fetch(weight, first, rows, pieces=4):
    return call(
        functools.partial(fetch_kernel, pieces, first),
        pltpu.VMEM((rows, weight.shape[1]), weight.dtype),
        pltpu.with_memory_space_constraint(weight, pltpu.HBM),
        scratch=[pltpu.SemaphoreType.DMA((pieces,))],
        specs=[HBM_SPEC],
        vmem=1 << 20,
    )


def factors_kernel(g_ref, u_ref, a_ref, b_ref, h_ref):
    g = g_ref[...].astype(f32)
    u = u_ref[...].astype(f32)
    q = 1.0 / (1.0 + jnp.exp(-g))
    b = g * q
    a_ref[...] = u * q * (1.0 + g * (1.0 - q))
    b_ref[...] = b
    h_ref[...] = (b * u).astype(bf16)


def split_terms(x):
    hi = x.astype(bf16)
    rest = x - hi.astype(f32)
    mid = rest.astype(bf16)
    low = (rest - mid.astype(f32)).astype(bf16)
    return hi, mid, low


def join_terms(hi, mid, low):
    return hi.astype(f32) + (mid.astype(f32) + low.astype(f32))


def store_terms(ref, start, x):
    n = x.shape[0]
    for i, term in enumerate(split_terms(x)):
        ref[start + i * n : start + (i + 1) * n, :] = term


def load_terms(ref, start, n):
    return join_terms(*(ref[start + i * n : start + (i + 1) * n, :] for i in range(3)))


def place_rows(full, pieces, position):
    n = pieces[0].shape[0]
    for k, piece in enumerate(pieces):
        full[pl.ds(pl.multiple_of((position ^ k) * n, n), n), :] = piece[...]


def hidden_block(full, low, w, entry, first, size):
    rows = pl.ds(pl.multiple_of(first, LANES), size)
    return contract_trailing(full[...], w[rows, :]) + adapter_scale * contract_leading(
        low, entry[:, rows].astype(f32), HIGHEST
    )


def send_kernel(half, block, o0, o1, o2, o3, w, exit_ref, entry, *outs):
    outs, low_ref, full = outs[:-2], outs[-2], outs[-1]
    n = outs[0].shape[0]
    place_rows(full, (o0, o1, o2, o3), lax.axis_index("row"))
    start = (1 - lax.rem(lax.axis_index("col"), 2)) * half
    low = contract_trailing(exit_ref[...], full[...])
    low_ref[...] = low
    outs[0][: low.shape[0], half:] = low
    for i in range(half // block):
        piece = hidden_block(full, low, w, entry, start + i * block, block)
        for j, out in enumerate(outs):
            out[:, i * block : (i + 1) * block] = piece[j * n : (j + 1) * n, :]


def keep_kernel(half, block, full, low, w, entry, out):
    start = lax.rem(lax.axis_index("col"), 2) * half
    for i in range(0, out.shape[1], block):
        size = min(block, out.shape[1] - i)
        out[:, i : i + size] = hidden_block(full, low[...], w, entry, start + i, size)


def store_blocks(out, piece, got, first):
    rows = piece.shape[0]
    for i in range(0, piece.shape[1], LANES):
        here = i // LANES * rows
        other = jnp.concatenate([ref[:, first + i : first + i + LANES] for ref in got], axis=0)
        out[here : here + rows, :] = (piece[:, i : i + LANES] + other).astype(bf16)


def payload_kernel(half, keep, low, *rest):
    got, out = rest[:-1], rest[-1]
    rank = low.shape[0]
    store_blocks(out, keep[...], got, 0)
    store_terms(out, out.shape[0] - 3 * rank, low[...] + got[0][:rank, half:])


def rest_kernel(half, first, full, low, w, entry, *rest):
    got, out = rest[:-1], rest[-1]
    start = lax.rem(lax.axis_index("col"), 2) * half + first
    piece = hidden_block(full, low[...], w, entry, start, half - first)
    store_blocks(out, piece, got, first)


def gradient_kernel(mine0, mine1, other0, other1, a, b, *outs):
    gate_outs, up_outs, low_ref = outs[:2], outs[2:4], outs[4]
    rows = a.shape[0]
    n, half = up_outs[0].shape
    rank = low_ref.shape[0]
    blocks = half // LANES
    later = mine1.shape[0] // rows
    start = pl.multiple_of(lax.rem(lax.axis_index("col"), 2) * half, half)
    for i in range(blocks):
        early = i < blocks - later
        k = i if early else i - (blocks - later)
        here = slice(k * rows, (k + 1) * rows)
        mine, other = (mine0, other0) if early else (mine1, other1)
        grad = mine[here, :].astype(f32) + other[here, :].astype(f32)
        lanes = pl.ds(pl.multiple_of(start + i * LANES, LANES), LANES)
        for refs, factor in ((gate_outs, a), (up_outs, b)):
            value = (grad * factor[:, lanes]).astype(bf16)
            for j, ref in enumerate(refs):
                ref[:, i * LANES : (i + 1) * LANES] = value[j * n : (j + 1) * n, :]
    terms = (blocks - later) * rows
    low_ref[...] = load_terms(mine0, terms, rank) + load_terms(other0, terms, rank)


def place_halves(full, own, mate):
    n, half = own[0].shape
    par = lax.rem(lax.axis_index("col"), 2)
    for position, refs in ((par, own), (1 - par, mate)):
        lanes = pl.ds(pl.multiple_of(position * half, half), half)
        for j, ref in enumerate(refs):
            full[j * n : (j + 1) * n, lanes] = ref[...]


def inputs_kernel(first, with_low, block, *refs):
    own, mate, (wg, wu, exit_ref, entry), rest = refs[:4], refs[4:8], refs[8:12], refs[12:]
    own_out, s1, s2, s3 = rest[:4]
    low_ref = rest[4] if with_low else None
    gg, ug, acc = rest[-3:]
    width = acc.shape[1]
    rank = exit_ref.shape[0]
    place_halves(gg, own[:2], mate[:2])
    place_halves(ug, own[2:], mate[2:])
    low = contract_trailing(exit_ref[...], ug[...])
    for i in range(width // block):
        rows = slice(i * block, (i + 1) * block)
        lanes = slice(first + i * block, first + (i + 1) * block)
        acc[:, i * block : (i + 1) * block] = (
            contract_trailing(gg[...], wg[rows, :])
            + contract_trailing(ug[...], wu[rows, :])
            + adapter_scale * contract_leading(low, entry[:, lanes].astype(f32), HIGHEST)
        )
    row = lax.axis_index("row")
    n = own_out.shape[0]
    own_out[...] = acc[pl.ds(pl.multiple_of(row * n, n), n), :]
    for k, out in ((1, s1), (2, s2), (3, s3)):
        dest = pl.ds(pl.multiple_of((row ^ k) * n, n), n)
        for i in range(width // LANES):
            out[i * n : (i + 1) * n, :] = acc[dest, i * LANES : (i + 1) * LANES].astype(bf16)
        if with_low:
            store_terms(out, width // LANES * n, low)
    if with_low:
        low_ref[...] = low


def finish_kernel(own, r1, r2, r3, *rest):
    done, out = rest[:-1], rest[-1]
    n, width = own.shape
    first = out.shape[1] - width
    for ref in done:
        out[:, :first] = ref[...]
    for i in range(width // LANES):
        here = slice(i * n, (i + 1) * n)
        lanes = slice(i * LANES, (i + 1) * LANES)
        out[:, first + i * LANES : first + (i + 1) * LANES] = (
            own[:, lanes]
            + r1[here, :].astype(f32)
            + r2[here, :].astype(f32)
            + r3[here, :].astype(f32)
        ).astype(bf16)


def entry_kernel(offset, low, r1, r2, r3, i0, i1, i2, i3, out, full, lows):
    row = lax.axis_index("row")
    rank = low.shape[0]
    place_rows(full, (i0, i1, i2, i3), row)
    lows[row] = low[...]
    for k, ref in ((1, r1), (2, r2), (3, r3)):
        lows[row ^ k] = load_terms(ref, offset, rank)
    total = (lows[0] + lows[1]) + (lows[2] + lows[3])
    whole = full[...]
    out[...] = adapter_scale * sum(
        jnp.dot(term, whole, preferred_element_type=f32) for term in split_terms(total)
    )


def small_kernel(own0, own1, mate0, mate1, low, hidden, up_act, down_act, full, *rest):
    up_exit, down_entry, down_exit, ug = rest
    place_halves(ug, (own0, own1), (mate0, mate1))
    up_exit[...] = adapter_scale * jnp.dot(up_act[...], ug[...], preferred_element_type=f32)
    down_entry[...] = adapter_scale * jnp.dot(
        low[...].astype(bf16), hidden[...], preferred_element_type=f32
    )
    down_exit[...] = adapter_scale * jnp.dot(down_act[...], full[...], preferred_element_type=f32)


def swap(x, axis, distance, n):
    return lax.ppermute(x, axis, [(i, i ^ distance) for i in range(n)])


EIGHTHS = (4,4)
CHUNKS = len(EIGHTHS)
KEEP_EIGHTHS = 5


def exchange_body(
    inputs,
    output_gradient,
    gate_preactivation,
    up_preactivation,
    gate_weight,
    up_weight,
    down_weight,
    up_adapter_entry,
    up_adapter_exit,
    down_adapter_entry,
    down_adapter_exit,
    up_adapter_activations,
    down_adapter_activations,
):
    tokens, hidden = gate_preactivation.shape
    share, width = output_gradient.shape
    rank = up_adapter_exit.shape[0]
    half = hidden // 2
    own_gradient = output_gradient
    gathered = [swap(own_gradient, "row", k, 4) for k in (1, 2)]
    parts = [width // 8 * e for e in EIGHTHS]
    firsts = [sum(parts[:c]) for c in range(CHUNKS)]
    down_v = fetch(down_weight, 0, hidden)
    gate_v = [fetch(gate_weight, firsts[c], parts[c]) for c in range(CHUNKS)]
    up_v = [fetch(up_weight, firsts[c], parts[c]) for c in range(CHUNKS - 1)]
    near = swap(inputs, "row", 1, 4)
    gathered.append(swap(after(gathered[1], gate_v, up_v, near), "row", 1, 4))
    down_v = after(down_v, gate_v, up_v, near)

    quarter = shape((tokens // 1, half + LANES), f32)
    *send, low_piece, full_gradient = call(
        functools.partial(send_kernel, half, 256),
        (quarter,) * 1 + (shape((rank, tokens), f32), shape((tokens, width), bf16)),
        own_gradient,
        *gathered,
        in_vmem(down_v),
        down_adapter_exit,
        down_adapter_entry,
    )
    got = [swap(x, "col", 1, 4) for x in send]
    far = swap(after(inputs, gathered, near), "row", 2, 4)
    last = swap(far, "row", 1, 4)
    first = half // 8 * KEEP_EIGHTHS
    keep = call(
        functools.partial(keep_kernel, half, 256),
        shape((tokens, first), f32),
        full_gradient,
        low_piece,
        in_vmem(down_v),
        down_adapter_entry,
    )
    early = call(
        functools.partial(payload_kernel, half),
        shape((first // LANES * tokens + 3 * rank, LANES), bf16),
        keep,
        low_piece,
        *got,
    )
    late = call(
        functools.partial(rest_kernel, half, first),
        shape(((half - first) // LANES * tokens, LANES), bf16),
        after(full_gradient, early),
        low_piece,
        in_vmem(down_v),
        down_adapter_entry,
        *got,
    )
    payload = (early, late)
    other = [swap(x, "col", 2, 4) for x in payload]
    up_v.append(fetch(after(up_weight, payload), firsts[-1], parts[-1]))
    a, b, hidden_state = call(
        factors_kernel,
        (shape((tokens, hidden), f32), shape((tokens, hidden), f32), shape((tokens, hidden), bf16)),
        after(gate_preactivation, payload),
        up_preactivation,
    )
    *grads, low_full = call(
        gradient_kernel,
        (shape((tokens // 2, half), bf16),) * 4 + (shape((rank, tokens), f32),),
        *payload,
        *other,
        after(a, up_v),
        b,
    )
    mate_grads = [swap(x, "col", 1, 4) for x in grads]

    owns, received = [], []
    outs = ()
    for c in range(CHUNKS):
        with_low = c == 0
        rows = parts[c] // LANES * share
        sent = shape((rows + (3 * rank if with_low else 0), LANES), bf16)
        outs = call(
            functools.partial(inputs_kernel, firsts[c], with_low, 512),
            (shape((share, parts[c]), f32), sent, sent, sent)
            + ((shape((rank, tokens), f32),) if with_low else ()),
            *grads,
            *mate_grads,
            in_vmem(after(gate_v[c], outs, last) if c else gate_v[c]),
            in_vmem(up_v[c]),
            up_adapter_exit,
            up_adapter_entry,
            scratch=[
                pltpu.VMEM((tokens, hidden), bf16),
                pltpu.VMEM((tokens, hidden), bf16),
                pltpu.VMEM((tokens, parts[c]), f32),
            ],
        )
        if with_low:
            low_up = outs[4]
        owns.append(outs[0])
        received.append([swap(outs[k], "row", k, 4) for k in (1, 2, 3)])
    input_grad = ()
    for c in range(CHUNKS):
        done = shape((share, firsts[c] + parts[c]), bf16)
        own = after(owns[c], owns[c + 1]) if c + 1 < CHUNKS else owns[c]
        input_grad = (call(finish_kernel, done, own, *received[c], *input_grad),)
    entry_sum = call(
        functools.partial(entry_kernel, parts[0] // LANES * share),
        shape((rank, width), f32),
        after(low_up, owns),
        *received[0],
        inputs,
        near,
        far,
        last,
        scratch=[pltpu.VMEM((tokens, width), bf16), pltpu.VMEM((4, rank, tokens), f32)],
    )
    up_exit_gradient, down_entry_gradient, down_exit_gradient = call(
        small_kernel,
        (shape((rank, hidden), f32), shape((rank, hidden), f32), shape((rank, width), f32)),
        *grads[2:],
        *mate_grads[2:],
        low_full,
        hidden_state,
        up_adapter_activations,
        down_adapter_activations,
        full_gradient,
        scratch=[pltpu.VMEM((tokens, hidden), bf16)],
    )
    return (
        input_grad[0],
        entry_sum,
        up_exit_gradient,
        down_entry_gradient,
        down_exit_gradient,
    )


def body(
    inputs,
    output_gradient,
    gate_preactivation,
    up_preactivation,
    gate_weight,
    up_weight,
    down_weight,
    up_adapter_entry,
    up_adapter_exit,
    down_adapter_entry,
    down_adapter_exit,
    up_adapter_activations,
    down_adapter_activations,
):
    highest_setting = HIGHEST
    complete_gradient = lax.all_gather(output_gradient, "row", axis=0, tiled=True)
    down_piece = contract_trailing(complete_gradient, down_adapter_exit)
    hidden_piece = contract_trailing(complete_gradient, down_weight)
    hidden_piece = hidden_piece + adapter_scale * jnp.dot(
        down_piece, down_adapter_entry.astype(f32), precision=highest_setting
    )
    hidden_gradient, down_full = lax.psum((hidden_piece, down_piece), "col")
    gate_f = gate_preactivation.astype(f32)
    up_f = up_preactivation.astype(f32)
    sigmoid_gate = jax.nn.sigmoid(gate_f)
    hidden_state = (gate_f * sigmoid_gate * up_f).astype(bf16)
    gate_grad = (
        hidden_gradient * up_f * sigmoid_gate * (1.0 + gate_f * (1.0 - sigmoid_gate))
    ).astype(bf16)
    up_gradient = (hidden_gradient * gate_f * sigmoid_gate).astype(bf16)
    down_rounded_value = down_full.astype(bf16)
    upper_piece = contract_trailing(up_gradient, up_adapter_exit)
    input_piece = contract_trailing(gate_grad, gate_weight) + contract_trailing(
        up_gradient, up_weight
    )
    input_piece = input_piece + adapter_scale * jnp.dot(
        upper_piece, up_adapter_entry.astype(f32), precision=highest_setting
    )
    input_grad, upper_full = (
        lax.psum_scatter(input_piece, "row", scatter_dimension=0, tiled=True),
        lax.psum_scatter(upper_piece, "row", scatter_dimension=0, tiled=True),
    )
    up_entry_term = adapter_scale * contract_leading(
        upper_full, inputs.astype(f32), matmul_accuracy=highest_setting
    )
    up_entry_gradient = lax.psum(up_entry_term, "row")
    up_exit_gradient = adapter_scale * jnp.dot(
        up_adapter_activations, up_gradient, preferred_element_type=f32
    )
    down_entry_gradient = adapter_scale * contract_leading(down_rounded_value, hidden_state)
    down_exit_gradient = adapter_scale * jnp.dot(
        down_adapter_activations, complete_gradient, preferred_element_type=f32
    )
    return (
        input_grad.astype(bf16),
        up_entry_gradient,
        up_exit_gradient,
        down_entry_gradient,
        down_exit_gradient,
    )


def solution(mesh):
    placed = (
        P(("grp", "row"), "col"),
        P(("grp", "row"), "col"),
        P("grp", "row"),
        P("grp", "row"),
        P("col", "row"),
        P("col", "row"),
        P("row", "col"),
        P(None, "col"),
        P(None, "row"),
        P(None, "row"),
        P(None, "col"),
        P(None, "grp"),
        P(None, "grp"),
    )
    exchange = mesh.shape["row"] == 4 and mesh.shape["col"] == 4
    return jax.shard_map(
        exchange_body if exchange else body,
        mesh=mesh,
        in_specs=placed,
        out_specs=(
            P(("grp", "row"), "col"),
            P("grp", "col"),
            P("grp", "row"),
            P("grp", "row"),
            P("grp", "col"),
        ),
        check_vma=False,
    )
```
